256 devices in a mesh: gx: 128 (over x, y, z), gy: 2 (over core).
Axes of the slice: x: 4, y: 4, z: 8, core: 2. Of those that a mesh axis runs over, the one named last changes fastest.
Arguments:
- fields: float32 [5, 1536, 32, 128], P(None, 'gx', 'gy'), may hold values from -1.5 to 6, as said below
- phase_map: int32 [1536, 32, 128], P('gx', 'gy'), may hold values from 0 to 1, as said below
- lagged_speed: float32 [1], replicated, may hold values from 7 to 17, as said below
- step_count: int32 [1], replicated, may hold values from 0 to 1023
Outputs:
- advanced: float32 [5, 1536, 32, 128], P(None, 'gx', 'gy')
- next_speed: float32 [1], replicated
The draws below stay inside these ranges and needn't reach their ends.
Inputs may be any that keep to these rules, and one draw needn't show every extreme that they name: `phase_map`: in each column (fixed first and second index) the cells below a level between 32 and 96, drawn per column, are 1 and the cells above it are 0. Density lies within 1 to 2 in cells of phase 0 and within 1 to 4 in cells of phase 1; the pressure P(fields) lies within 0.6 to 1.6 and every velocity m_k / rho within -0.3 to 0.3. lagged_speed[0] lies between 1.01 and 1.31 times the largest over all cells of fields of |v_1| + |v_2| + |v_3| + 3 sqrt(gamma_cell (P + pinf_cell) / rho).
All inputs are finite; a program needn't handle non-finite values.
Results may differ from the reference program's by a relative error of at most 0.00002.
Values sent between devices are 32-bit elements; how exact they have to be, the bound alone decides.
A program may use at most 128 MiB of HBM per device.

```python
import math
import jax
import jax.numpy as jnp

PERIOD = 64
NX = 1536
NY = 32
NZ = 128


def column_phase(key):
    levels = jax.random.randint(jax.random.fold_in(key, 11), (NX, NY, 1), NZ // 4, 3 * NZ // 4 + 1)
    height = jnp.arange(NZ, dtype=jnp.int32).reshape(1, 1, NZ)
    return (height < levels).astype(jnp.int32)


def drawn_state(key):
    water_frac = column_phase(key).astype(jnp.float32)
    subkeys = jax.random.split(jax.random.fold_in(key, 12), 5)
    grid_shape = (NX, NY, NZ)
    first_hot = jax.random.randint(subkeys[3], (), 0, NX)
    offset = (jnp.arange(NX, dtype=jnp.int32) - first_hot) % NX
    inside = (offset < max(NX // 32, 1)).astype(jnp.float32).reshape(NX, 1, 1)
    heat = 1.05 + 0.1 * jax.random.uniform(subkeys[4], ())
    water_level = 2.0 / (1.0 + inside * (heat * heat - 1.0))
    density = (1.0 + jax.random.uniform(subkeys[0], grid_shape)) * (1.0 + water_frac * (water_level - 1.0))
    press_now = 0.6 + jax.random.uniform(subkeys[1], grid_shape)
    velocity = 0.3 * jax.random.uniform(subkeys[2], (3,) + grid_shape, minval=-1.0, maxval=1.0)
    return (water_frac, density, press_now, velocity)


def draw_phase_map(key, part):
    return column_phase(key)


def draw_fields(key, part):
    water_frac, density, press_now, velocity = drawn_state(key)
    gamma_cell = 1.4 + 3.0 * water_frac
    pinf_cell = 3.0 * water_frac
    kinetic = 0.5 * density * jnp.sum(velocity * velocity, axis=0)
    energy = (press_now + gamma_cell * pinf_cell) / (gamma_cell - 1.0) + kinetic
    momentum = density * velocity
    return jnp.stack([density, momentum[0], momentum[1], momentum[2], energy])


def draw_lagged_speed(key, part):
    water_frac, density, press_now, velocity = drawn_state(key)
    gamma_cell = 1.4 + 3.0 * water_frac
    pinf_cell = 3.0 * water_frac
    speed = jnp.sum(jnp.abs(velocity), axis=0) + 3.0 * jnp.sqrt(gamma_cell * (press_now + pinf_cell) / density)
    margin = 1.01 + 0.3 * jax.random.uniform(jax.random.fold_in(key, 13), ())
    return jnp.reshape(jnp.max(speed) * margin, (1,))


def setup_inputs(seed: int = 0) -> dict:
    arg_keys = jax.random.split(jax.random.key(seed), 5)
    fields = draw_fields(jax.random.fold_in(arg_keys[4], 71), 0)
    phase_map = draw_phase_map(jax.random.fold_in(arg_keys[4], 71), 0)
    lagged_speed = draw_lagged_speed(jax.random.fold_in(arg_keys[4], 71), 0)
    step_count = jax.random.randint(arg_keys[3], (1,), 0, 16 * PERIOD).astype(jnp.int32)
    return {"fields": fields, "phase_map": phase_map, "lagged_speed": lagged_speed, "step_count": step_count}


gamma_air = 1.4
gamma_water = 4.4
pinf_water = 3.0
cfl_number = 0.9
gravity = 1.0
shake_amp = 0.8
two_pi = 2.0 * math.pi
coef_one = 0.75
coef_two = -0.15
coef_three = 1.0 / 60.0
one_third = 1.0 / 3.0
two_thirds = 2.0 / 3.0

def pressure(fields, gamma_cell, pinf_cell):
    inverse = 1.0 / fields[0]
    kinetic = 0.5 * (fields[1] * (fields[1] * inverse) + fields[2] * (fields[2] * inverse) + fields[3] * (fields[3] * inverse))
    return (gamma_cell - 1.0) * (fields[4] - kinetic) - gamma_cell * pinf_cell

def fluxes(fields, press_now, direction):
    inverse = 1.0 / fields[0]
    velocity = fields[1 + direction] * inverse
    pieces = [fields[1 + direction]]
    for member in range(3):
        moment = fields[1 + member] * velocity
        if member == direction:
            moment = moment + press_now
        pieces.append(moment)
    pieces.append((fields[4] + press_now) * velocity)
    return jnp.stack(pieces)

def roll_one(values, along):

    def shifted(offset):
        return jnp.roll(values, -offset, along)
    return coef_one * (shifted(1) - shifted(-1)) + coef_two * (shifted(2) - shifted(-2)) + coef_three * (shifted(3) - shifted(-3))

def slope_roll(values, along):
    return jnp.stack([roll_one(values[member], along - 1) for member in range(values.shape[0])])

def sources(fields, gravity_now):
    blank = jnp.zeros_like(fields[0])
    return jnp.stack([blank, blank, blank, fields[0] * gravity_now, fields[3] * gravity_now])

def section_rates(fields, gamma_cell, pinf_cell, gravity_now):
    press_now = pressure(fields, gamma_cell, pinf_cell)
    divergence = slope_roll(fluxes(fields, press_now, 0), 1) + slope_roll(fluxes(fields, press_now, 1), 2)
    divergence = divergence + slope_roll(fluxes(fields, press_now, 2), 3)
    return sources(fields, gravity_now) - divergence

def top_speed(fields, gamma_cell, pinf_cell):
    press_now = pressure(fields, gamma_cell, pinf_cell)
    inverse = 1.0 / fields[0]
    local_speed = jnp.abs(fields[1] * inverse) + jnp.abs(fields[2] * inverse) + jnp.abs(fields[3] * inverse)
    local_speed = local_speed + 3.0 * jnp.sqrt(gamma_cell * (press_now + pinf_cell) * inverse)
    return jnp.max(local_speed)

def reference(fields, phase_map, lagged_speed, step_count):
    water_frac = phase_map.astype(jnp.float32)
    gamma_cell = gamma_air + (gamma_water - gamma_air) * water_frac
    pinf_cell = pinf_water * water_frac
    time_step = cfl_number / lagged_speed[0]
    gravity_now = gravity * (1.0 + shake_amp * jnp.cos(two_pi * step_count[0].astype(jnp.float32) / PERIOD))
    section_one = fields + time_step * section_rates(fields, gamma_cell, pinf_cell, gravity_now)
    section_two = 0.75 * fields + 0.25 * (section_one + time_step * section_rates(section_one, gamma_cell, pinf_cell, gravity_now))
    advanced = one_third * fields + two_thirds * (section_two + time_step * section_rates(section_two, gamma_cell, pinf_cell, gravity_now))
    return (advanced, jnp.reshape(top_speed(advanced, gamma_cell, pinf_cell), (1,)))
```

```python
import functools
import math

import jax
import jax.numpy as jnp
from jax import lax
from jax.experimental import pallas as pl
from jax.experimental.pallas import tpu as pltpu
from jax.sharding import Mesh
from jax.sharding import PartitionSpec as P

PERIOD = 64
DIMS = (4, 4, 8)
AXES = ("gx_0", "gx_1", "gx_2", "gy")
GX = AXES[:3]
MESH = pl.DeviceIdType.MESH

PLANES = 12
HALF = 6
HALO = 9
SLOTS = 18
COEFS = (0.75, -0.15, 1.0 / 60.0)


def slope(values, axis):
    size = values.shape[axis]
    total = None
    for d, coef in enumerate(COEFS, 1):
        term = coef * (pltpu.roll(values, size - d, axis) - pltpu.roll(values, d, axis))
        total = term if total is None else total + term
    return total


def cosine_of_step(step):
    u = (step % PERIOD - PERIOD // 2).astype(jnp.float32) * (2.0 * math.pi / PERIOD)
    half = 0.5 * u
    square = half * half
    sine = jnp.full_like(u, 0.0)
    for n in range(8, -1, -1):
        sine = sine * square + (-1.0) ** n / math.factorial(2 * n + 1)
    sine = sine * half
    return 2.0 * sine * sine - 1.0


def kernel(
    dims,
    fields, phase_map, lagged_speed, step_count,
    advanced, next_speed,
    state, flux, side, gam_one, gam_pinf, final, phases, own_level, levels,
    speed_s, step_s, best, best_sib, best_src, best_all,
    loc_sem, halo_send, halo_recv, sib_send, sib_recv, lev_send, lev_recv,
    cut_send, cut_recv, out_sem, out_send, out_recv, one_send, one_recv, all_send, all_recv, know,
):
    nx, ny, nz = dims
    x, y, z, c = (lax.axis_index(a) for a in AXES)
    s = 1 - c
    chips = nx * ny * nz
    g = (x * ny + y) * nz + z

    def chip(index):
        return (index // (ny * nz), lax.rem(index // nz, ny), lax.rem(index, nz))

    right = chip(lax.rem(g + 1, chips))
    left = chip(lax.rem(g + chips - 1, chips))
    me_sib = (x, y, z, s)

    column = [(x, y, lax.rem(z + d, nz), lax.rem(c + e, 2)) for d in range(nz) for e in range(2) if d or e]
    layer = [(lax.rem(x + d, nx), lax.rem(y + e, ny), z, c) for d in range(nx) for e in range(ny) if d or e]
    beside = [(*right, 0), (*right, 1), (*left, 0), (*left, 1)]

    barrier = pltpu.get_barrier_semaphore()
    peers = beside + column + layer
    for peer in peers:
        pl.semaphore_signal(barrier, inc=1, device_id=peer, device_id_type=MESH)

    row0 = pl.multiple_of(16 * c, 16)
    raw = state.at[0]
    copies = [
        pltpu.make_async_copy(phase_map, phases, loc_sem.at[0]),
        pltpu.make_async_copy(
            fields.at[:, pl.ds(3 * c, HALO)],
            raw.at[:, pl.ds(9 - 9 * c, HALO), pl.ds(row0, 16), :],
            loc_sem.at[1],
        ),
        pltpu.make_async_copy(lagged_speed, speed_s, loc_sem.at[2]),
        pltpu.make_async_copy(step_count, step_s, loc_sem.at[3]),
    ]
    for copy in copies:
        copy.start()
    copies[0].wait()
    lane = lax.broadcasted_iota(jnp.int32, (16, 128), 1)
    tile = jnp.zeros((16, 128), jnp.float32)
    for p in range(PLANES):
        level = jnp.sum(phases[p].astype(jnp.float32), axis=1, keepdims=True)
        tile = jnp.where(lane == p, level, tile)
    own_level[...] = tile

    pl.semaphore_wait(barrier, len(peers))

    rows = pl.ds(row0, 16)
    level_copies = [
        pltpu.make_async_remote_copy(
            own_level, levels.at[n, rows, :], lev_send.at[i], lev_recv.at[n, c], device_id=dev, device_id_type=MESH
        )
        for i, (n, dev) in enumerate(((0, me_sib), (1, (*right, 0)), (1, (*left, 1))))
    ]
    for copy in level_copies:
        copy.start()
    sib_copy = pltpu.make_async_remote_copy(
        fields.at[:, pl.ds(3 * s, HALO)],
        raw.at[:, pl.ds(9 - 9 * s, HALO), rows, :],
        sib_send.at[0],
        sib_recv.at[0],
        device_id=me_sib,
        device_id_type=MESH,
    )

    def halo_copy(i, way):
        src, slot, dev = ((11 - i, 8 - i, (*right, 0)), (i, 9 + i, (*left, 1)))[way]
        return pltpu.make_async_remote_copy(
            fields.at[:, pl.ds(src, 1)],
            raw.at[:, pl.ds(slot, 1), rows, :],
            halo_send.at[i, way],
            halo_recv.at[i, c],
            device_id=dev,
            device_id_type=MESH,
        )

    for way in range(2):
        halo_copy(0, way).start()
    sib_copy.start()
    for i in range(1, HALO):
        for way in range(2):
            halo_copy(i, way).start()
    for peer in layer:
        pl.semaphore_signal(know, inc=1, device_id=peer, device_id_type=MESH)

    copies[2].wait()
    copies[3].wait()
    time_step = 0.9 / jnp.full((8, 128), speed_s[0], jnp.float32)
    gravity = 1.0 + 0.8 * cosine_of_step(jnp.full((8, 128), step_s[0], jnp.int32))
    time_step = jnp.concatenate([time_step] * 4, axis=0)
    gravity = jnp.concatenate([gravity] * 4, axis=0)

    lane32 = lax.broadcasted_iota(jnp.int32, (32, 128), 1)

    def slot_of(k):
        return 14 - k + c * (2 * k - 11)

    def set_gamma(k, n, plane):
        chosen = jnp.where(lane32 == plane, levels[n], 0.0)
        level = jnp.sum(chosen, axis=1, keepdims=True)
        water = jnp.where(lane32.astype(jnp.float32) < level, 1.0, 0.0)
        gamma = 1.4 + 3.0 * water
        j = slot_of(k)
        gam_one[j] = gamma - 1.0
        gam_pinf[j] = gamma * (3.0 * water)

    def primitives(section, j):
        rho, m1, m2, m3, energy = (state[section, f, j] for f in range(5))
        inverse = 1.0 / rho
        v1, v2, v3 = m1 * inverse, m2 * inverse, m3 * inverse
        kinetic = 0.5 * (m1 * v1 + m2 * v2 + m3 * v3)
        press = gam_one[j] * (energy - kinetic) - gam_pinf[j]
        return rho, (m1, m2, m3), (v1, v2, v3), press, energy + press

    def put_flux(section, j, moments, speeds, press, total):
        m1, m2, m3 = moments
        v1 = speeds[0]
        flux[section, 0, j] = m1
        flux[section, 1, j] = m1 * v1 + press
        flux[section, 2, j] = m2 * v1
        flux[section, 3, j] = m3 * v1
        flux[section, 4, j] = total * v1

    def flux_only(section, k):
        j = slot_of(k)
        _, moments, speeds, press, total = primitives(section, j)
        put_flux(section, j, moments, speeds, press, total)

    def flux_and_side(section, k):
        j = slot_of(k)
        rho, moments, speeds, press, total = primitives(section, j)
        put_flux(section, j, moments, speeds, press, total)
        m1, m2, m3 = moments
        _, v2, v3 = speeds
        side[section, 0, j] = slope(m2, 0) + slope(m3, 1)
        side[section, 1, j] = slope(m1 * v2, 0) + slope(m1 * v3, 1)
        cross = m3 * v2
        side[section, 2, j] = slope(m2 * v2 + press, 0) + slope(cross, 1)
        side[section, 3, j] = slope(cross, 0) + slope(m3 * v3 + press, 1) - rho * gravity
        side[section, 4, j] = slope(total * v2, 0) + slope(total * v3, 1) - m3 * gravity

    def rate(section, f, j):
        total = side[section, f, j]
        for d, coef in enumerate(COEFS, 1):
            total = total + coef * (flux[section, f, j + d] - flux[section, f, j - d])
        return total

    def update_one(k):
        j = slot_of(k)
        for f in range(5):
            state[1, f, j] = state[0, f, j] - time_step * rate(0, f, j)

    def update_two(k):
        j = slot_of(k)
        for f in range(5):
            state[2, f, j] = 0.75 * state[0, f, j] + 0.25 * (state[1, f, j] - time_step * rate(1, f, j))

    def update_three(k):
        j = slot_of(k)
        out = []
        for f in range(5):
            new = (1.0 / 3.0) * state[0, f, j] + (2.0 / 3.0) * (state[2, f, j] - time_step * rate(2, f, j))
            final[f, (1 - c) * (5 - k) + c * k] = new
            out.append(new)
        rho, m1, m2, m3, energy = out
        inverse = 1.0 / rho
        v1, v2, v3 = m1 * inverse, m2 * inverse, m3 * inverse
        kinetic = 0.5 * (m1 * v1 + m2 * v2 + m3 * v3)
        one, both = gam_one[j], gam_pinf[j]
        gamma = one + 1.0
        press = one * (energy - kinetic) - both
        speed = jnp.abs(v1) + jnp.abs(v2) + jnp.abs(v3)
        speed = speed + 3.0 * jnp.sqrt((gamma * press + both) * inverse)
        best[...] = jnp.maximum(best[...], jnp.maximum(jnp.maximum(speed[:8], speed[8:16]), jnp.maximum(speed[16:24], speed[24:])))

    def cut_copy(section, start_here, start_there):
        return pltpu.make_async_remote_copy(
            flux.at[section, :, pl.ds(start_here, 3)],
            flux.at[section, :, pl.ds(start_there, 3)],
            cut_send.at[section],
            cut_recv.at[section],
            device_id=me_sib,
            device_id_type=MESH,
        )

    def cut(section):
        return cut_copy(section, 12 - 9 * c, 15 * c)

    best[...] = jnp.zeros((8, 128), jnp.float32)
    levels_own = pltpu.make_async_copy(own_level, levels.at[0, rows, :], loc_sem.at[4])
    levels_own.start()
    levels_own.wait()
    level_wait = lambda n, core: pltpu.make_async_remote_copy(
        own_level, levels.at[n, pl.ds(0, 16), :], lev_send.at[0], lev_recv.at[n, core], device_id=me_sib, device_id_type=MESH
    ).wait_recv()
    level_wait(0, s)
    copies[1].wait()
    sib_copy.wait_recv()

    @pl.loop(-3, 6)
    def _(k):
        set_gamma(k, 0, (1 - c) * (5 - k) + c * (6 + k))

    @pl.loop(-3, 0)
    def _(k):
        flux_only(0, k)

    @pl.loop(0, 3)
    def _(k):
        flux_and_side(0, k)

    @pl.loop(3, 15)
    def _(k):
        @pl.when(k == 6)
        def _():
            level_wait(1, 0)
            level_wait(1, 1)

        @pl.when(k >= 6)
        def _():
            for core in range(2):
                pltpu.make_async_remote_copy(
                    fields.at[:, pl.ds(0, 1)],
                    raw.at[:, pl.ds(0, 1), pl.ds(0, 16), :],
                    halo_send.at[0, 0],
                    halo_recv.at[k - 6, core],
                    device_id=me_sib,
                    device_id_type=MESH,
                ).wait_recv()
            set_gamma(k, 1, (1 - c) * (17 - k) + c * (k - 6))

        @pl.when(k < 12)
        def _():
            flux_and_side(0, k)

        @pl.when(k >= 12)
        def _():
            flux_only(0, k)

        update_one(k - 3)

        @pl.when(k < 12)
        def _():
            flux_and_side(1, k - 3)

        @pl.when(k >= 12)
        def _():
            flux_only(1, k - 3)

        @pl.when(k == 5)
        def _():
            cut(1).start()

        @pl.when(k == 6)
        def _():
            cut(1).wait_recv()

        @pl.when(k >= 6)
        def _():
            update_two(k - 6)

            @pl.when(k < 12)
            def _():
                flux_and_side(2, k - 6)

            @pl.when(k >= 12)
            def _():
                flux_only(2, k - 6)

        @pl.when(k == 8)
        def _():
            cut(2).start()

        @pl.when(k == 9)
        def _():
            cut(2).wait_recv()

        @pl.when(k >= 9)
        def _():
            update_three(k - 9)

    best_src[0] = jnp.max(best[...], axis=0, keepdims=True)
    one = pltpu.make_async_remote_copy(
        best_src.at[0], best_sib, one_send.at[0], one_recv.at[0], device_id=me_sib, device_id_type=MESH
    )
    one.start()
    pl.semaphore_wait(know, len(layer))
    one.wait_recv()
    best_src[1] = jnp.maximum(best_src[0], best_sib[...])

    offsets = [(a, b, d) for a in range(nx) for b in range(ny) for d in range(nz)][1:]
    far = lambda o: -(min(o[0], nx - o[0]) + min(o[1], ny - o[1]) + min(o[2], nz - o[2]))
    offsets.sort(key=far)
    for i, (a, b, d) in enumerate(offsets):
        pltpu.make_async_remote_copy(
            best_src.at[1],
            best_all.at[i],
            all_send.at[0],
            all_recv.at[0],
            device_id=(lax.rem(x + a, nx), lax.rem(y + b, ny), lax.rem(z + d, nz), c),
            device_id_type=MESH,
        ).start()

    keep = pltpu.make_async_copy(
        final.at[:, :, rows, :], advanced.at[:, pl.ds(HALF * c, HALF)], out_sem.at[0]
    )
    keep.start()
    give = pltpu.make_async_remote_copy(
        final.at[:, :, pl.ds(pl.multiple_of(16 * s, 16), 16), :],
        advanced.at[:, pl.ds(HALF * c, HALF)],
        out_send.at[0],
        out_recv.at[0],
        device_id=me_sib,
        device_id_type=MESH,
    )
    give.start()

    for copy in level_copies:
        copy.wait_send()
    sib_copy.wait_send()
    for i in range(HALO):
        for way in range(2):
            halo_copy(i, way).wait_send()
    cut(1).wait_send()
    cut(2).wait_send()
    one.wait_send()
    keep.wait()
    give.wait()

    everything = pltpu.make_async_remote_copy(
        best_all, best_all, all_send.at[0], all_recv.at[0], device_id=me_sib, device_id_type=MESH
    )
    everything.wait_recv()
    largest = jnp.maximum(best_src[1], jnp.max(best_all[...], axis=0))
    next_speed[0] = jnp.max(largest)
    everything.wait_send()


def solution(mesh, dims=DIMS):
    cores = mesh.shape["gy"]
    finer = Mesh(mesh.devices.reshape(*dims, cores), AXES)
    chips = dims[0] * dims[1] * dims[2]
    dma = pltpu.SemaphoreType.DMA
    f32 = jnp.float32

    def local(fields, phase_map, lagged_speed, step_count):
        return pl.pallas_call(
            functools.partial(kernel, dims),
            out_shape=(
                jax.ShapeDtypeStruct(fields.shape, f32),
                jax.ShapeDtypeStruct((1,), f32),
            ),
            in_specs=[pl.BlockSpec(memory_space=pl.ANY)] * 4,
            out_specs=(pl.BlockSpec(memory_space=pl.ANY), pl.BlockSpec(memory_space=pltpu.SMEM)),
            scratch_shapes=[
                pltpu.VMEM((3, 5, SLOTS, 32, 128), f32),
                pltpu.VMEM((3, 5, SLOTS, 32, 128), f32),
                pltpu.VMEM((3, 5, SLOTS, 32, 128), f32),
                pltpu.VMEM((SLOTS, 32, 128), f32),
                pltpu.VMEM((SLOTS, 32, 128), f32),
                pltpu.VMEM((5, HALF, 32, 128), f32),
                pltpu.VMEM((PLANES, 16, 128), jnp.int32),
                pltpu.VMEM((16, 128), f32),
                pltpu.VMEM((2, 32, 128), f32),
                pltpu.SMEM((1,), f32),
                pltpu.SMEM((1,), jnp.int32),
                pltpu.VMEM((8, 128), f32),
                pltpu.VMEM((1, 128), f32),
                pltpu.VMEM((2, 1, 128), f32),
                pltpu.VMEM((chips - 1, 1, 128), f32),
                dma((5,)),
                dma((HALO, 2)),
                dma((HALO, 2)),
                dma((1,)),
                dma((1,)),
                dma((3,)),
                dma((2, 2)),
                dma((3,)),
                dma((3,)),
                dma((1,)),
                dma((1,)),
                dma((1,)),
                dma((1,)),
                dma((1,)),
                dma((1,)),
                dma((1,)),
                pltpu.SemaphoreType.REGULAR,
            ],
            compiler_params=pltpu.CompilerParams(
                collective_id=0, has_side_effects=True, vmem_limit_bytes=32 << 20
            ),
            name="step",
        )(fields, phase_map, lagged_speed, step_count)

    in_specs = (P(None, GX, "gy", None), P(GX, "gy", None), P(), P())
    out_specs = (P(None, GX, "gy", None), P())
    return jax.shard_map(local, mesh=finer, in_specs=in_specs, out_specs=out_specs, check_vma=False)
```

```python
import functools
import math

import jax
import jax.numpy as jnp
from jax import lax
from jax.experimental import pallas as pl
from jax.experimental.pallas import tpu as pltpu
from jax.sharding import Mesh
from jax.sharding import PartitionSpec as P

PERIOD = 64
DIMS = (4, 4, 8)
AXES = ("gx_0", "gx_1", "gx_2", "gy")
GX = AXES[:3]
MESH = pl.DeviceIdType.MESH

PLANES = 12
HALF = 6
HALO = 9
SLOTS = 18
COEFS = (0.75, -0.15, 1.0 / 60.0)


def slope(values, axis):
    size = values.shape[axis]
    total = None
    for d, coef in enumerate(COEFS, 1):
        term = coef * (pltpu.roll(values, size - d, axis) - pltpu.roll(values, d, axis))
        total = term if total is None else total + term
    return total


def cosine_of_step(step):
    u = (step % PERIOD - PERIOD // 2).astype(jnp.float32) * (2.0 * math.pi / PERIOD)
    half = 0.5 * u
    square = half * half
    sine = jnp.full_like(u, 0.0)
    for n in range(8, -1, -1):
        sine = sine * square + (-1.0) ** n / math.factorial(2 * n + 1)
    sine = sine * half
    return 2.0 * sine * sine - 1.0


def kernel(
    dims,
    fields, phase_map, lagged_speed, step_count,
    advanced, next_speed,
    state, flux, side, gam_one, gam_pinf, final, partial, phases, own_level, levels,
    speed_s, step_s, best, best_sib, best_src, best_all,
    loc_sem, halo_send, halo_recv, sib_send, sib_recv, lev_send, lev_recv,
    cut_send, cut_recv, out_sem, out_send, out_recv, one_send, one_recv, all_send, all_recv, know,
):
    nx, ny, nz = dims
    x, y, z, c = (lax.axis_index(a) for a in AXES)
    s = 1 - c
    chips = nx * ny * nz
    g = (x * ny + y) * nz + z

    def chip(index):
        return (index // (ny * nz), lax.rem(index // nz, ny), lax.rem(index, nz))

    right = chip(lax.rem(g + 1, chips))
    left = chip(lax.rem(g + chips - 1, chips))
    me_sib = (x, y, z, s)

    beside = [(*right, 0), (*right, 1), (*left, 0), (*left, 1)]
    steps = ((1, 0, 0), (nx - 1, 0, 0), (0, 1, 0), (0, ny - 1, 0), (0, 0, 1), (0, 0, nz - 1))

    def away(a, b, d):
        return (lax.rem(x + a, nx), lax.rem(y + b, ny), lax.rem(z + d, nz), c)

    rounds = (
        [away(*step) for step in steps],
        [away(0, 0, 2 % nz), away(0, 0, (nz - 2) % nz)],
        [away(d, 0, 0) for d in range(1, nx)],
        [away(0, d, 0) for d in range(1, ny)],
    )

    def tell(i):
        for peer in rounds[i]:
            pl.semaphore_signal(know.at[i], inc=1, device_id=peer, device_id_type=MESH)

    def hear(i):
        pl.semaphore_wait(know.at[i], len(rounds[i]))

    barrier = pltpu.get_barrier_semaphore()
    peers = beside + [me_sib] + rounds[0]
    for peer in peers:
        pl.semaphore_signal(barrier, inc=1, device_id=peer, device_id_type=MESH)

    row0 = pl.multiple_of(16 * c, 16)
    raw = state.at[0]
    copies = [
        pltpu.make_async_copy(phase_map, phases, loc_sem.at[0]),
        pltpu.make_async_copy(
            fields.at[:, pl.ds(3 * c, HALO)],
            raw.at[:, pl.ds(9 - 9 * c, HALO), pl.ds(row0, 16), :],
            loc_sem.at[1],
        ),
        pltpu.make_async_copy(lagged_speed, speed_s, loc_sem.at[2]),
        pltpu.make_async_copy(step_count, step_s, loc_sem.at[3]),
    ]
    for copy in copies:
        copy.start()
    copies[0].wait()
    lane = lax.broadcasted_iota(jnp.int32, (16, 128), 1)
    tile = jnp.zeros((16, 128), jnp.float32)
    for p in range(PLANES):
        level = jnp.sum(phases[p].astype(jnp.float32), axis=1, keepdims=True)
        tile = jnp.where(lane == p, level, tile)
    own_level[...] = tile

    pl.semaphore_wait(barrier, len(peers))

    rows = pl.ds(row0, 16)
    level_copies = [
        pltpu.make_async_remote_copy(
            own_level, levels.at[n, rows, :], lev_send.at[i], lev_recv.at[n, c], device_id=dev, device_id_type=MESH
        )
        for i, (n, dev) in enumerate(((0, me_sib), (1, (*right, 0)), (1, (*left, 1))))
    ]
    for copy in level_copies:
        copy.start()
    sib_copy = pltpu.make_async_remote_copy(
        fields.at[:, pl.ds(3 * s, HALO)],
        raw.at[:, pl.ds(9 - 9 * s, HALO), rows, :],
        sib_send.at[0],
        sib_recv.at[0],
        device_id=me_sib,
        device_id_type=MESH,
    )

    def halo_copy(i, toward):
        src, slot, dev = ((11 - i, 8 - i, (*right, 0)), (i, 9 + i, (*left, 1)))[toward]
        return pltpu.make_async_remote_copy(
            fields.at[:, pl.ds(src, 1)],
            raw.at[:, pl.ds(slot, 1), rows, :],
            halo_send.at[i, toward],
            halo_recv.at[i, c],
            device_id=dev,
            device_id_type=MESH,
        )

    for toward in range(2):
        halo_copy(0, toward).start()
    sib_copy.start()
    for i in range(1, HALO):
        for toward in range(2):
            halo_copy(i, toward).start()
    tell(0)

    copies[2].wait()
    copies[3].wait()
    time_step = 0.9 / jnp.full((8, 128), speed_s[0], jnp.float32)
    gravity = 1.0 + 0.8 * cosine_of_step(jnp.full((8, 128), step_s[0], jnp.int32))
    time_step = jnp.concatenate([time_step] * 4, axis=0)
    gravity = jnp.concatenate([gravity] * 4, axis=0)
    way = 2 * c - 1
    time_way = time_step * way.astype(jnp.float32)

    lane32 = lax.broadcasted_iota(jnp.int32, (32, 128), 1)

    def slot_of(k):
        return 14 - k + c * (2 * k - 11)

    def set_gamma(k, n, plane):
        chosen = jnp.where(lane32 == plane, levels[n], 0.0)
        level = jnp.sum(chosen, axis=1, keepdims=True)
        water = jnp.where(lane32.astype(jnp.float32) < level, 1.0, 0.0)
        gamma = 1.4 + 3.0 * water
        j = slot_of(k)
        gam_one[j] = gamma - 1.0
        gam_pinf[j] = gamma * (3.0 * water)

    def primitives(section, j):
        rho, m1, m2, m3, energy = (state[section, f, j] for f in range(5))
        inverse = 1.0 / rho
        v1, v2, v3 = m1 * inverse, m2 * inverse, m3 * inverse
        kinetic = 0.5 * (m1 * v1 + m2 * v2 + m3 * v3)
        press = gam_one[j] * (energy - kinetic) - gam_pinf[j]
        return rho, (m1, m2, m3), (v1, v2, v3), press, energy + press

    def first_flux(section, j):
        _, (m1, m2, m3), (v1, _, _), press, total = primitives(section, j)
        values = (m1, m1 * v1 + press, m2 * v1, m3 * v1, total * v1)
        for f in range(5):
            flux[section, f, j] = values[f]
        return values

    def side_of(section, j):
        rho, (m1, m2, m3), (_, v2, v3), press, total = primitives(section, j)
        side[section, 0, j] = slope(m2, 0) + slope(m3, 1)
        side[section, 1, j] = slope(m1 * v2, 0) + slope(m1 * v3, 1)
        cross = m3 * v2
        side[section, 2, j] = slope(m2 * v2 + press, 0) + slope(cross, 1)
        side[section, 3, j] = slope(cross, 0) + slope(m3 * v3 + press, 1) - rho * gravity
        side[section, 4, j] = slope(total * v2, 0) + slope(total * v3, 1) - m3 * gravity

    def begin(section, k):
        j = slot_of(k)
        for f in range(5):
            slope_one = -COEFS[2] * flux[section, f, j - 3 * way]
            for d in (1, 2):
                slope_one = slope_one + COEFS[d - 1] * (flux[section, f, j + d * way] - flux[section, f, j - d * way])
            new = state[section, f, j] - time_step * side[section, f, j] - time_way * slope_one
            if section == 1:
                new = 0.75 * state[0, f, j] + 0.25 * new
            if section == 2:
                new = (1.0 / 3.0) * state[0, f, j] + (2.0 / 3.0) * new
            partial[section, f] = new

    weights = (1.0, 0.25, 2.0 / 3.0)

    def finish(section, values):
        scale = (weights[section] * COEFS[2]) * time_way
        return [partial[section, f] - scale * values[f] for f in range(5)]

    def store_state(section, j, values):
        for f in range(5):
            state[section, f, j] = values[f]

    def store_final(k, out):
        j = slot_of(k)
        for f in range(5):
            final[f, (1 - c) * (5 - k) + c * k] = out[f]
        rho, m1, m2, m3, energy = out
        inverse = 1.0 / rho
        v1, v2, v3 = m1 * inverse, m2 * inverse, m3 * inverse
        kinetic = 0.5 * (m1 * v1 + m2 * v2 + m3 * v3)
        one, both = gam_one[j], gam_pinf[j]
        press = one * (energy - kinetic) - both
        speed = jnp.abs(v1) + jnp.abs(v2) + jnp.abs(v3)
        speed = speed + 3.0 * jnp.sqrt(((one + 1.0) * press + both) * inverse)
        speed = jnp.maximum(jnp.maximum(speed[:8], speed[8:16]), jnp.maximum(speed[16:24], speed[24:]))
        best[...] = jnp.maximum(best[...], speed)

    def step(k, fetched, sections, sides):
        for section in range(sections):
            begin(section, k - 3 - 3 * section)
        if fetched:
            for core in range(2):
                pltpu.make_async_remote_copy(
                    fields.at[:, pl.ds(0, 1)],
                    raw.at[:, pl.ds(0, 1), pl.ds(0, 16), :],
                    halo_send.at[0, 0],
                    halo_recv.at[k - 6, core],
                    device_id=me_sib,
                    device_id_type=MESH,
                ).wait_recv()
        values = first_flux(0, slot_of(k))
        for section in range(sections):
            inner = k - 3 - 3 * section
            new = finish(section, values)
            if section == 2:
                store_final(inner, new)
            else:
                store_state(section + 1, slot_of(inner), new)
                values = first_flux(section + 1, slot_of(inner))
        if sides:
            for section in range(min(sections + 1, 3)):
                side_of(section, slot_of(k - 3 * section))

    def cut_copy(section, start_here, start_there):
        return pltpu.make_async_remote_copy(
            flux.at[section, :, pl.ds(start_here, 3)],
            flux.at[section, :, pl.ds(start_there, 3)],
            cut_send.at[section],
            cut_recv.at[section],
            device_id=me_sib,
            device_id_type=MESH,
        )

    def cut(section):
        return cut_copy(section, 12 - 9 * c, 15 * c)

    best[...] = jnp.zeros((8, 128), jnp.float32)
    levels_own = pltpu.make_async_copy(own_level, levels.at[0, rows, :], loc_sem.at[4])
    levels_own.start()
    levels_own.wait()
    level_wait = lambda n, core: pltpu.make_async_remote_copy(
        own_level, levels.at[n, pl.ds(0, 16), :], lev_send.at[0], lev_recv.at[n, core], device_id=me_sib, device_id_type=MESH
    ).wait_recv()
    level_wait(0, s)
    copies[1].wait()
    sib_copy.wait_recv()

    @pl.loop(-3, 6)
    def _(k):
        set_gamma(k, 0, (1 - c) * (5 - k) + c * (6 + k))

    @pl.loop(-3, 0)
    def _(k):
        first_flux(0, slot_of(k))

    @pl.loop(0, 3)
    def _(k):
        first_flux(0, slot_of(k))
        side_of(0, slot_of(k))

    hear(0)
    tell(1)

    @pl.loop(3, 6)
    def _(k):
        step(k, False, 1, True)

    cut(1).start()
    level_wait(1, 0)
    level_wait(1, 1)

    @pl.loop(6, 15)
    def _(k):
        set_gamma(k, 1, (1 - c) * (17 - k) + c * (k - 6))

    hear(1)
    tell(2)
    cut(1).wait_recv()

    @pl.loop(6, 9)
    def _(k):
        step(k, True, 2, True)

    cut(2).start()
    hear(2)
    tell(3)
    cut(2).wait_recv()

    @pl.loop(9, 12)
    def _(k):
        step(k, True, 3, True)

    @pl.loop(12, 15)
    def _(k):
        step(k, True, 3, False)

    best_src[0] = jnp.max(best[...], axis=0, keepdims=True)
    one = pltpu.make_async_remote_copy(
        best_src.at[0], best_sib, one_send.at[0], one_recv.at[0], device_id=me_sib, device_id_type=MESH
    )
    one.start()
    hear(3)
    one.wait_recv()
    best_src[1] = jnp.maximum(best_src[0], best_sib[...])

    offsets = [(a, b, d) for a in range(nx) for b in range(ny) for d in range(nz)][1:]
    far = lambda o: -(min(o[0], nx - o[0]) + min(o[1], ny - o[1]) + min(o[2], nz - o[2]))
    offsets.sort(key=far)
    for i, (a, b, d) in enumerate(offsets):
        pltpu.make_async_remote_copy(
            best_src.at[1],
            best_all.at[i],
            all_send.at[0],
            all_recv.at[0],
            device_id=(lax.rem(x + a, nx), lax.rem(y + b, ny), lax.rem(z + d, nz), c),
            device_id_type=MESH,
        ).start()

    keep = pltpu.make_async_copy(
        final.at[:, :, rows, :], advanced.at[:, pl.ds(HALF * c, HALF)], out_sem.at[0]
    )
    keep.start()
    give = pltpu.make_async_remote_copy(
        final.at[:, :, pl.ds(pl.multiple_of(16 * s, 16), 16), :],
        advanced.at[:, pl.ds(HALF * c, HALF)],
        out_send.at[0],
        out_recv.at[0],
        device_id=me_sib,
        device_id_type=MESH,
    )
    give.start()

    for copy in level_copies:
        copy.wait_send()
    sib_copy.wait_send()
    for i in range(HALO):
        for toward in range(2):
            halo_copy(i, toward).wait_send()
    cut(1).wait_send()
    cut(2).wait_send()
    one.wait_send()
    keep.wait()
    give.wait()

    everything = pltpu.make_async_remote_copy(
        best_all, best_all, all_send.at[0], all_recv.at[0], device_id=me_sib, device_id_type=MESH
    )
    everything.wait_recv()
    largest = jnp.maximum(best_src[1], jnp.max(best_all[...], axis=0))
    next_speed[...] = jnp.broadcast_to(jnp.max(largest, axis=1, keepdims=True), (1, 128))
    everything.wait_send()


def keep_kernel(adv, spd, adv_out, spd_out, spd_s, sem):
    one = pltpu.make_async_copy(adv, adv_out, sem.at[0])
    spd_s[0] = spd[0, 0]
    two = pltpu.make_async_copy(spd_s, spd_out, sem.at[1])
    one.start(); two.start(); one.wait(); two.wait()


def solution(mesh, dims=DIMS):
    cores = mesh.shape["gy"]
    finer = Mesh(mesh.devices.reshape(*dims, cores), AXES)
    chips = dims[0] * dims[1] * dims[2]
    dma = pltpu.SemaphoreType.DMA
    f32 = jnp.float32

    def local(fields, phase_map, lagged_speed, step_count):
        adv, spd = pl.pallas_call(
            functools.partial(kernel, dims),
            out_shape=(
                jax.ShapeDtypeStruct(fields.shape, f32),
                jax.ShapeDtypeStruct((1, 128), f32),
            ),
            in_specs=[pl.BlockSpec(memory_space=pl.ANY)] * 4,
            out_specs=(pl.BlockSpec(memory_space=pl.ANY), pl.BlockSpec(memory_space=pltpu.VMEM)),
            scratch_shapes=[
                pltpu.VMEM((3, 5, SLOTS, 32, 128), f32),
                pltpu.VMEM((3, 5, SLOTS, 32, 128), f32),
                pltpu.VMEM((3, 5, SLOTS, 32, 128), f32),
                pltpu.VMEM((SLOTS, 32, 128), f32),
                pltpu.VMEM((SLOTS, 32, 128), f32),
                pltpu.VMEM((5, HALF, 32, 128), f32),
                pltpu.VMEM((3, 5, 32, 128), f32),
                pltpu.VMEM((PLANES, 16, 128), jnp.int32),
                pltpu.VMEM((16, 128), f32),
                pltpu.VMEM((2, 32, 128), f32),
                pltpu.SMEM((1,), f32),
                pltpu.SMEM((1,), jnp.int32),
                pltpu.VMEM((8, 128), f32),
                pltpu.VMEM((1, 128), f32),
                pltpu.VMEM((2, 1, 128), f32),
                pltpu.VMEM((chips - 1, 1, 128), f32),
                dma((5,)),
                dma((HALO, 2)),
                dma((HALO, 2)),
                dma((1,)),
                dma((1,)),
                dma((3,)),
                dma((2, 2)),
                dma((3,)),
                dma((3,)),
                dma((1,)),
                dma((1,)),
                dma((1,)),
                dma((1,)),
                dma((1,)),
                dma((1,)),
                dma((1,)),
                pltpu.SemaphoreType.REGULAR((4,)),
            ],
            compiler_params=pltpu.CompilerParams(
                collective_id=0, has_side_effects=True, vmem_limit_bytes=32 << 20
            ),
            name="step",
        )(pltpu.with_memory_space_constraint(fields, pltpu.HBM), pltpu.with_memory_space_constraint(phase_map, pltpu.HBM), lagged_speed, step_count)
        return pl.pallas_call(
            keep_kernel,
            out_shape=(jax.ShapeDtypeStruct(fields.shape, f32), jax.ShapeDtypeStruct((1,), f32)),
            in_specs=[pl.BlockSpec(memory_space=pl.ANY), pl.BlockSpec(memory_space=pltpu.VMEM)],
            out_specs=(pl.BlockSpec(memory_space=pltpu.HBM), pl.BlockSpec(memory_space=pltpu.HBM)),
            scratch_shapes=[pltpu.SMEM((1,), f32), dma((2,))],
            compiler_params=pltpu.CompilerParams(vmem_limit_bytes=1 << 20),
            name="keep",
        )(adv, spd)

    in_specs = (P(None, GX, "gy", None), P(GX, "gy", None), P(), P())
    out_specs = (P(None, GX, "gy", None), P())
    return jax.shard_map(local, mesh=finer, in_specs=in_specs, out_specs=out_specs, check_vma=False)
```

```python
import functools
import math

import jax
import jax.numpy as jnp
from jax import lax
from jax.experimental import pallas as pl
from jax.experimental.pallas import tpu as pltpu
from jax.sharding import Mesh
from jax.sharding import PartitionSpec as P

PERIOD = 64
DIMS = (4, 4, 8)
AXES = ("gx_0", "gx_1", "gx_2", "gy")
GX = AXES[:3]
MESH = pl.DeviceIdType.MESH

PLANES = 12
HALF = 6
HALO = 9
SLOTS = 18
COEFS = (0.75, -0.15, 1.0 / 60.0)


def slope(values, axis):
    size = values.shape[axis]
    total = None
    for d, coef in enumerate(COEFS, 1):
        term = coef * (pltpu.roll(values, size - d, axis) - pltpu.roll(values, d, axis))
        total = term if total is None else total + term
    return total


def cosine_of_step(step):
    u = (step % PERIOD - PERIOD // 2).astype(jnp.float32) * (2.0 * math.pi / PERIOD)
    half = 0.5 * u
    square = half * half
    sine = jnp.full_like(u, 0.0)
    for n in range(8, -1, -1):
        sine = sine * square + (-1.0) ** n / math.factorial(2 * n + 1)
    sine = sine * half
    return 2.0 * sine * sine - 1.0


def kernel(
    dims,
    fields, phase_map, lagged_speed, step_count,
    advanced, next_speed,
    state, flux, side, gam_one, gam_pinf, final, partial, phases, own_level, levels,
    speed_s, step_s, best, best_sib, best_src, best_all,
    loc_sem, halo_send, halo_recv, sib_send, sib_recv, lev_send, lev_recv,
    cut_send, cut_recv, out_sem, out_send, out_recv, one_send, one_recv, all_send, all_recv, know,
):
    nx, ny, nz = dims
    x, y, z, c = (lax.axis_index(a) for a in AXES)
    s = 1 - c
    chips = nx * ny * nz
    g = (x * ny + y) * nz + z

    def chip(index):
        return (index // (ny * nz), lax.rem(index // nz, ny), lax.rem(index, nz))

    right = chip(lax.rem(g + 1, chips))
    left = chip(lax.rem(g + chips - 1, chips))
    me_sib = (x, y, z, s)

    steps = ((1, 0, 0), (nx - 1, 0, 0), (0, 1, 0), (0, ny - 1, 0), (0, 0, 1), (0, 0, nz - 1))

    def away(a, b, d):
        return (lax.rem(x + a, nx), lax.rem(y + b, ny), lax.rem(z + d, nz), c)

    rounds = (
        [away(*step) for step in steps],
        [away(0, 0, 2 % nz), away(0, 0, (nz - 2) % nz)],
        [away(d, 0, 0) for d in range(1, nx)],
        [away(0, d, 0) for d in range(1, ny)],
    )

    def tell(i):
        for peer in rounds[i]:
            pl.semaphore_signal(know.at[i], inc=1, device_id=peer, device_id_type=MESH)

    def hear(i):
        pl.semaphore_wait(know.at[i], len(rounds[i]))

    barrier = pltpu.get_barrier_semaphore()
    mine = tuple(c * r + s * l for r, l in zip(right, left))
    peers = [(*mine, 0), (*mine, 1), me_sib] + rounds[0]
    for peer in peers:
        pl.semaphore_signal(barrier, inc=1, device_id=peer, device_id_type=MESH)

    row0 = pl.multiple_of(16 * c, 16)
    raw = state.at[0]
    copies = [
        pltpu.make_async_copy(phase_map, phases, loc_sem.at[0]),
        pltpu.make_async_copy(
            fields.at[:, pl.ds(3 * c, HALO)],
            raw.at[:, pl.ds(9 - 9 * c, HALO), pl.ds(row0, 16), :],
            loc_sem.at[1],
        ),
        pltpu.make_async_copy(lagged_speed, speed_s, loc_sem.at[2]),
        pltpu.make_async_copy(step_count, step_s, loc_sem.at[3]),
    ]
    for copy in copies:
        copy.start()
    copies[0].wait()
    lane = lax.broadcasted_iota(jnp.int32, (16, 128), 1)
    tile = jnp.zeros((16, 128), jnp.float32)
    for p in range(PLANES):
        level = jnp.sum(phases[p].astype(jnp.float32), axis=1, keepdims=True)
        tile = jnp.where(lane == p, level, tile)
    own_level[...] = tile

    pl.semaphore_wait(barrier, len(peers))

    rows = pl.ds(row0, 16)
    level_copies = [
        pltpu.make_async_remote_copy(
            own_level, levels.at[n, rows, :], lev_send.at[i], lev_recv.at[n, c], device_id=dev, device_id_type=MESH
        )
        for i, (n, dev) in enumerate(((0, me_sib), (1, (*right, 0)), (1, (*left, 1))))
    ]
    for copy in level_copies:
        copy.start()
    sib_copy = pltpu.make_async_remote_copy(
        fields.at[:, pl.ds(3 * s, HALO)],
        raw.at[:, pl.ds(9 - 9 * s, HALO), rows, :],
        sib_send.at[0],
        sib_recv.at[0],
        device_id=me_sib,
        device_id_type=MESH,
    )

    def halo_copy(i, toward):
        src, slot, dev = ((11 - i, 8 - i, (*right, 0)), (i, 9 + i, (*left, 1)))[toward]
        return pltpu.make_async_remote_copy(
            fields.at[:, pl.ds(src, 1)],
            raw.at[:, pl.ds(slot, 1), rows, :],
            halo_send.at[i, toward],
            halo_recv.at[i, c],
            device_id=dev,
            device_id_type=MESH,
        )

    for toward in range(2):
        halo_copy(0, toward).start()
    sib_copy.start()
    for i in range(1, HALO):
        for toward in range(2):
            halo_copy(i, toward).start()
    tell(0)

    copies[2].wait()
    copies[3].wait()
    time_step = 0.9 / jnp.full((8, 128), speed_s[0], jnp.float32)
    gravity = 1.0 + 0.8 * cosine_of_step(jnp.full((8, 128), step_s[0], jnp.int32))
    time_step = jnp.concatenate([time_step] * 4, axis=0)
    gravity = jnp.concatenate([gravity] * 4, axis=0)
    way = 2 * c - 1
    time_way = time_step * way.astype(jnp.float32)

    lane32 = lax.broadcasted_iota(jnp.int32, (32, 128), 1)

    def slot_of(k):
        return 14 - k + c * (2 * k - 11)

    def set_gamma(k, n, plane):
        chosen = jnp.where(lane32 == plane, levels[n], 0.0)
        level = jnp.sum(chosen, axis=1, keepdims=True)
        water = jnp.where(lane32.astype(jnp.float32) < level, 1.0, 0.0)
        gamma = 1.4 + 3.0 * water
        j = slot_of(k)
        gam_one[j] = gamma - 1.0
        gam_pinf[j] = gamma * (3.0 * water)

    def primitives(section, j):
        rho, m1, m2, m3, energy = (state[section, f, j] for f in range(5))
        inverse = 1.0 / rho
        v1, v2, v3 = m1 * inverse, m2 * inverse, m3 * inverse
        kinetic = 0.5 * (m1 * v1 + m2 * v2 + m3 * v3)
        press = gam_one[j] * (energy - kinetic) - gam_pinf[j]
        return rho, (m1, m2, m3), (v1, v2, v3), press, energy + press

    def first_flux(section, j):
        _, (m1, m2, m3), (v1, _, _), press, total = primitives(section, j)
        values = (m1, m1 * v1 + press, m2 * v1, m3 * v1, total * v1)
        for f in range(5):
            flux[section, f, j] = values[f]
        return values

    def side_of(section, j):
        rho, (m1, m2, m3), (_, v2, v3), press, total = primitives(section, j)
        side[section, 0, j] = slope(m2, 0) + slope(m3, 1)
        side[section, 1, j] = slope(m1 * v2, 0) + slope(m1 * v3, 1)
        cross = m3 * v2
        side[section, 2, j] = slope(m2 * v2 + press, 0) + slope(cross, 1)
        side[section, 3, j] = slope(cross, 0) + slope(m3 * v3 + press, 1) - rho * gravity
        side[section, 4, j] = slope(total * v2, 0) + slope(total * v3, 1) - m3 * gravity

    def begin(section, k):
        j = slot_of(k)
        for f in range(5):
            slope_one = -COEFS[2] * flux[section, f, j - 3 * way]
            for d in (1, 2):
                slope_one = slope_one + COEFS[d - 1] * (flux[section, f, j + d * way] - flux[section, f, j - d * way])
            new = state[section, f, j] - time_step * side[section, f, j] - time_way * slope_one
            if section == 1:
                new = 0.75 * state[0, f, j] + 0.25 * new
            if section == 2:
                new = (1.0 / 3.0) * state[0, f, j] + (2.0 / 3.0) * new
            partial[section, f] = new

    weights = (1.0, 0.25, 2.0 / 3.0)

    def finish(section, values):
        scale = (weights[section] * COEFS[2]) * time_way
        return [partial[section, f] - scale * values[f] for f in range(5)]

    def store_state(section, j, values):
        for f in range(5):
            state[section, f, j] = values[f]

    def store_final(k, out):
        j = slot_of(k)
        for f in range(5):
            final[f, (1 - c) * (5 - k) + c * k] = out[f]
        rho, m1, m2, m3, energy = out
        inverse = 1.0 / rho
        v1, v2, v3 = m1 * inverse, m2 * inverse, m3 * inverse
        kinetic = 0.5 * (m1 * v1 + m2 * v2 + m3 * v3)
        one, both = gam_one[j], gam_pinf[j]
        press = one * (energy - kinetic) - both
        speed = jnp.abs(v1) + jnp.abs(v2) + jnp.abs(v3)
        speed = speed + 3.0 * jnp.sqrt(((one + 1.0) * press + both) * inverse)
        speed = jnp.maximum(jnp.maximum(speed[:8], speed[8:16]), jnp.maximum(speed[16:24], speed[24:]))
        best[...] = jnp.maximum(best[...], speed)

    def step(k, fetched, sections, sides):
        for section in range(sections):
            begin(section, k - 3 - 3 * section)
        if fetched:
            for core in range(2):
                pltpu.make_async_remote_copy(
                    fields.at[:, pl.ds(0, 1)],
                    raw.at[:, pl.ds(0, 1), pl.ds(0, 16), :],
                    halo_send.at[0, 0],
                    halo_recv.at[k - 6, core],
                    device_id=me_sib,
                    device_id_type=MESH,
                ).wait_recv()
        values = first_flux(0, slot_of(k))
        for section in range(sections):
            inner = k - 3 - 3 * section
            new = finish(section, values)
            if section == 2:
                store_final(inner, new)
            else:
                store_state(section + 1, slot_of(inner), new)
                values = first_flux(section + 1, slot_of(inner))
        if sides:
            for section in range(min(sections + 1, 3)):
                side_of(section, slot_of(k - 3 * section))

    def cut_copy(section, start_here, start_there):
        return pltpu.make_async_remote_copy(
            flux.at[section, :, pl.ds(start_here, 3)],
            flux.at[section, :, pl.ds(start_there, 3)],
            cut_send.at[section],
            cut_recv.at[section],
            device_id=me_sib,
            device_id_type=MESH,
        )

    def cut(section):
        return cut_copy(section, 12 - 9 * c, 15 * c)

    best[...] = jnp.zeros((8, 128), jnp.float32)
    levels_own = pltpu.make_async_copy(own_level, levels.at[0, rows, :], loc_sem.at[4])
    levels_own.start()
    levels_own.wait()
    level_wait = lambda n, core: pltpu.make_async_remote_copy(
        own_level, levels.at[n, pl.ds(0, 16), :], lev_send.at[0], lev_recv.at[n, core], device_id=me_sib, device_id_type=MESH
    ).wait_recv()
    level_wait(0, s)
    copies[1].wait()
    sib_copy.wait_recv()

    @pl.loop(-3, 6)
    def _(k):
        set_gamma(k, 0, (1 - c) * (5 - k) + c * (6 + k))

    @pl.loop(-3, 0)
    def _(k):
        first_flux(0, slot_of(k))

    @pl.loop(0, 3)
    def _(k):
        first_flux(0, slot_of(k))
        side_of(0, slot_of(k))

    hear(0)
    tell(1)

    @pl.loop(3, 6)
    def _(k):
        step(k, False, 1, True)

    cut(1).start()
    level_wait(1, 0)
    level_wait(1, 1)

    @pl.loop(6, 15)
    def _(k):
        set_gamma(k, 1, (1 - c) * (17 - k) + c * (k - 6))

    hear(1)
    tell(2)
    cut(1).wait_recv()

    @pl.loop(6, 9)
    def _(k):
        step(k, True, 2, True)

    cut(2).start()
    hear(2)
    tell(3)
    cut(2).wait_recv()

    @pl.loop(9, 12)
    def _(k):
        step(k, True, 3, True)

    @pl.loop(12, 15)
    def _(k):
        step(k, True, 3, False)

    best_src[0] = jnp.max(best[...], axis=0, keepdims=True)
    one = pltpu.make_async_remote_copy(
        best_src.at[0], best_sib, one_send.at[0], one_recv.at[0], device_id=me_sib, device_id_type=MESH
    )
    one.start()
    hear(3)
    one.wait_recv()
    best_src[1] = jnp.maximum(best_src[0], best_sib[...])

    offsets = [(a, b, d) for a in range(nx) for b in range(ny) for d in range(nz)][1:]
    far = lambda o: -(min(o[0], nx - o[0]) + min(o[1], ny - o[1]) + min(o[2], nz - o[2]))
    offsets.sort(key=far)
    for i, (a, b, d) in enumerate(offsets):
        pltpu.make_async_remote_copy(
            best_src.at[1],
            best_all.at[i],
            all_send.at[0],
            all_recv.at[0],
            device_id=(lax.rem(x + a, nx), lax.rem(y + b, ny), lax.rem(z + d, nz), c),
            device_id_type=MESH,
        ).start()

    keep = pltpu.make_async_copy(
        final.at[:, :, rows, :], advanced.at[:, pl.ds(HALF * c, HALF)], out_sem.at[0]
    )
    keep.start()
    give = pltpu.make_async_remote_copy(
        final.at[:, :, pl.ds(pl.multiple_of(16 * s, 16), 16), :],
        advanced.at[:, pl.ds(HALF * c, HALF)],
        out_send.at[0],
        out_recv.at[0],
        device_id=me_sib,
        device_id_type=MESH,
    )
    give.start()

    for copy in level_copies:
        copy.wait_send()
    sib_copy.wait_send()
    for i in range(HALO):
        for toward in range(2):
            halo_copy(i, toward).wait_send()
    cut(1).wait_send()
    cut(2).wait_send()
    one.wait_send()
    keep.wait()
    give.wait()

    everything = pltpu.make_async_remote_copy(
        best_all, best_all, all_send.at[0], all_recv.at[0], device_id=me_sib, device_id_type=MESH
    )
    everything.wait_recv()
    largest = jnp.maximum(best_src[1], jnp.max(best_all[...], axis=0))
    next_speed[...] = jnp.broadcast_to(jnp.max(largest, axis=1, keepdims=True), (1, 128))
    everything.wait_send()


def keep_kernel(adv, spd, adv_out, spd_out, spd_s, sem):
    one = pltpu.make_async_copy(adv, adv_out, sem.at[0])
    spd_s[0] = spd[0, 0]
    two = pltpu.make_async_copy(spd_s, spd_out, sem.at[1])
    one.start(); two.start(); one.wait(); two.wait()


def solution(mesh, dims=DIMS):
    cores = mesh.shape["gy"]
    finer = Mesh(mesh.devices.reshape(*dims, cores), AXES)
    chips = dims[0] * dims[1] * dims[2]
    dma = pltpu.SemaphoreType.DMA
    f32 = jnp.float32

    def local(fields, phase_map, lagged_speed, step_count):
        adv, spd = pl.pallas_call(
            functools.partial(kernel, dims),
            out_shape=(
                jax.ShapeDtypeStruct(fields.shape, f32),
                jax.ShapeDtypeStruct((1, 128), f32),
            ),
            in_specs=[pl.BlockSpec(memory_space=pl.ANY)] * 4,
            out_specs=(pl.BlockSpec(memory_space=pl.ANY), pl.BlockSpec(memory_space=pltpu.VMEM)),
            scratch_shapes=[
                pltpu.VMEM((3, 5, SLOTS, 32, 128), f32),
                pltpu.VMEM((3, 5, SLOTS, 32, 128), f32),
                pltpu.VMEM((3, 5, SLOTS, 32, 128), f32),
                pltpu.VMEM((SLOTS, 32, 128), f32),
                pltpu.VMEM((SLOTS, 32, 128), f32),
                pltpu.VMEM((5, HALF, 32, 128), f32),
                pltpu.VMEM((3, 5, 32, 128), f32),
                pltpu.VMEM((PLANES, 16, 128), jnp.int32),
                pltpu.VMEM((16, 128), f32),
                pltpu.VMEM((2, 32, 128), f32),
                pltpu.SMEM((1,), f32),
                pltpu.SMEM((1,), jnp.int32),
                pltpu.VMEM((8, 128), f32),
                pltpu.VMEM((1, 128), f32),
                pltpu.VMEM((2, 1, 128), f32),
                pltpu.VMEM((chips - 1, 1, 128), f32),
                dma((5,)),
                dma((HALO, 2)),
                dma((HALO, 2)),
                dma((1,)),
                dma((1,)),
                dma((3,)),
                dma((2, 2)),
                dma((3,)),
                dma((3,)),
                dma((1,)),
                dma((1,)),
                dma((1,)),
                dma((1,)),
                dma((1,)),
                dma((1,)),
                dma((1,)),
                pltpu.SemaphoreType.REGULAR((4,)),
            ],
            compiler_params=pltpu.CompilerParams(
                collective_id=0, has_side_effects=True, vmem_limit_bytes=32 << 20
            ),
            name="step",
        )(pltpu.with_memory_space_constraint(fields, pltpu.HBM), pltpu.with_memory_space_constraint(phase_map, pltpu.HBM), lagged_speed, step_count)
        return pl.pallas_call(
            keep_kernel,
            out_shape=(jax.ShapeDtypeStruct(fields.shape, f32), jax.ShapeDtypeStruct((1,), f32)),
            in_specs=[pl.BlockSpec(memory_space=pl.ANY), pl.BlockSpec(memory_space=pltpu.VMEM)],
            out_specs=(pl.BlockSpec(memory_space=pltpu.HBM), pl.BlockSpec(memory_space=pltpu.HBM)),
            scratch_shapes=[pltpu.SMEM((1,), f32), dma((2,))],
            compiler_params=pltpu.CompilerParams(vmem_limit_bytes=1 << 20),
            name="keep",
        )(adv, spd)

    in_specs = (P(None, GX, "gy", None), P(GX, "gy", None), P(), P())
    out_specs = (P(None, GX, "gy", None), P())
    return jax.shard_map(local, mesh=finer, in_specs=in_specs, out_specs=out_specs, check_vma=False)
```

```python
import functools
import math

import jax
import jax.numpy as jnp
from jax import lax
from jax.experimental import pallas as pl
from jax.experimental.pallas import tpu as pltpu
from jax.sharding import Mesh
from jax.sharding import PartitionSpec as P

PERIOD = 64
DIMS = (4, 4, 8)
AXES = ("gx_0", "gx_1", "gx_2", "gy")
GX = AXES[:3]
MESH = pl.DeviceIdType.MESH

PLANES = 12
HALF = 6
HALO = 9
SLOTS = 18
COEFS = (0.75, -0.15, 1.0 / 60.0)


def slope(values, axis):
    size = values.shape[axis]
    total = None
    for d, coef in enumerate(COEFS, 1):
        term = coef * (pltpu.roll(values, size - d, axis) - pltpu.roll(values, d, axis))
        total = term if total is None else total + term
    return total


def cosine_of_step(step):
    u = (step % PERIOD - PERIOD // 2).astype(jnp.float32) * (2.0 * math.pi / PERIOD)
    half = 0.5 * u
    square = half * half
    sine = jnp.full_like(u, 0.0)
    for n in range(8, -1, -1):
        sine = sine * square + (-1.0) ** n / math.factorial(2 * n + 1)
    sine = sine * half
    return 2.0 * sine * sine - 1.0


def kernel(
    dims,
    fields, phase_map, lagged_speed, step_count,
    advanced, next_speed,
    state, flux, side, gam_one, gam_pinf, final, partial, phases, own_level, levels,
    speed_s, step_s, best, best_sib, best_src, best_all,
    loc_sem, halo_send, halo_recv, sib_send, sib_recv, lev_send, lev_recv,
    cut_send, cut_recv, out_sem, out_send, out_recv, one_send, one_recv, all_send, all_recv, know,
):
    nx, ny, nz = dims
    x, y, z, c = (lax.axis_index(a) for a in AXES)
    s = 1 - c
    chips = nx * ny * nz
    g = (x * ny + y) * nz + z

    def chip(index):
        return (index // (ny * nz), lax.rem(index // nz, ny), lax.rem(index, nz))

    right = chip(lax.rem(g + 1, chips))
    left = chip(lax.rem(g + chips - 1, chips))
    me_sib = (x, y, z, s)

    steps = ((1, 0, 0), (nx - 1, 0, 0), (0, 1, 0), (0, ny - 1, 0), (0, 0, 1), (0, 0, nz - 1))

    def away(a, b, d):
        return (lax.rem(x + a, nx), lax.rem(y + b, ny), lax.rem(z + d, nz), c)

    rounds = (
        [away(*step) for step in steps],
        [away(0, 0, 2 % nz), away(0, 0, (nz - 2) % nz)],
        [away(d, 0, 0) for d in range(1, nx)],
        [away(0, d, 0) for d in range(1, ny)],
    )

    def tell(i):
        for peer in rounds[i]:
            pl.semaphore_signal(know.at[i], inc=1, device_id=peer, device_id_type=MESH)

    def hear(i):
        pl.semaphore_wait(know.at[i], len(rounds[i]))

    barrier = pltpu.get_barrier_semaphore()
    mine = tuple(c * r + s * l for r, l in zip(right, left))
    peers = [(*mine, 0), (*mine, 1), me_sib] + rounds[0]
    for peer in peers:
        pl.semaphore_signal(barrier, inc=1, device_id=peer, device_id_type=MESH)

    row0 = pl.multiple_of(16 * c, 16)
    raw = state.at[0]
    copies = [
        pltpu.make_async_copy(phase_map, phases, loc_sem.at[0]),
        pltpu.make_async_copy(
            fields.at[:, pl.ds(3 * c, HALO)],
            raw.at[:, pl.ds(9 - 9 * c, HALO), pl.ds(row0, 16), :],
            loc_sem.at[1],
        ),
        pltpu.make_async_copy(lagged_speed, speed_s, loc_sem.at[2]),
        pltpu.make_async_copy(step_count, step_s, loc_sem.at[3]),
    ]
    for copy in copies:
        copy.start()
    copies[0].wait()
    lane = lax.broadcasted_iota(jnp.int32, (16, 128), 1)
    tile = jnp.zeros((16, 128), jnp.float32)
    for p in range(PLANES):
        level = jnp.sum(phases[p].astype(jnp.float32), axis=1, keepdims=True)
        tile = jnp.where(lane == p, level, tile)
    own_level[...] = tile

    pl.semaphore_wait(barrier, len(peers))

    rows = pl.ds(row0, 16)
    level_copies = [
        pltpu.make_async_remote_copy(
            own_level, levels.at[n, rows, :], lev_send.at[i], lev_recv.at[n, c], device_id=dev, device_id_type=MESH
        )
        for i, (n, dev) in enumerate(((0, me_sib), (1, (*right, 0)), (1, (*left, 1))))
    ]
    for copy in level_copies:
        copy.start()
    sib_copy = pltpu.make_async_remote_copy(
        fields.at[:, pl.ds(3 * s, HALO)],
        raw.at[:, pl.ds(9 - 9 * s, HALO), rows, :],
        sib_send.at[0],
        sib_recv.at[0],
        device_id=me_sib,
        device_id_type=MESH,
    )

    def halo_copy(i, toward):
        src, slot, dev = ((11 - i, 8 - i, (*right, 0)), (i, 9 + i, (*left, 1)))[toward]
        return pltpu.make_async_remote_copy(
            fields.at[:, pl.ds(src, 1)],
            raw.at[:, pl.ds(slot, 1), rows, :],
            halo_send.at[i, toward],
            halo_recv.at[i, c],
            device_id=dev,
            device_id_type=MESH,
        )

    for toward in range(2):
        halo_copy(0, toward).start()
    sib_copy.start()
    for i in range(1, HALO):
        for toward in range(2):
            halo_copy(i, toward).start()
    tell(0)

    copies[2].wait()
    copies[3].wait()
    time_step = 0.9 / jnp.full((8, 128), speed_s[0], jnp.float32)
    gravity = 1.0 + 0.8 * cosine_of_step(jnp.full((8, 128), step_s[0], jnp.int32))
    time_step = jnp.concatenate([time_step] * 4, axis=0)
    gravity = jnp.concatenate([gravity] * 4, axis=0)
    way = 2 * c - 1
    time_way = time_step * way.astype(jnp.float32)

    lane32 = lax.broadcasted_iota(jnp.int32, (32, 128), 1)

    def slot_of(k):
        return 14 - k + c * (2 * k - 11)

    def set_gamma(k, n, plane):
        chosen = jnp.where(lane32 == plane, levels[n], 0.0)
        level = jnp.sum(chosen, axis=1, keepdims=True)
        water = jnp.where(lane32.astype(jnp.float32) < level, 1.0, 0.0)
        gamma = 1.4 + 3.0 * water
        j = slot_of(k)
        gam_one[j] = gamma - 1.0
        gam_pinf[j] = gamma * (3.0 * water)

    def primitives(section, j):
        rho, m1, m2, m3, energy = (state[section, f, j] for f in range(5))
        inverse = 1.0 / rho
        v1, v2, v3 = m1 * inverse, m2 * inverse, m3 * inverse
        kinetic = 0.5 * (m1 * v1 + m2 * v2 + m3 * v3)
        press = gam_one[j] * (energy - kinetic) - gam_pinf[j]
        return rho, (m1, m2, m3), (v1, v2, v3), press, energy + press

    def first_flux(section, j):
        _, (m1, m2, m3), (v1, _, _), press, total = primitives(section, j)
        values = (m1, m1 * v1 + press, m2 * v1, m3 * v1, total * v1)
        for f in range(5):
            flux[section, f, j] = values[f]
        return values

    def side_of(section, j):
        rho, (m1, m2, m3), (_, v2, v3), press, total = primitives(section, j)
        side[section, 0, j] = slope(m2, 0) + slope(m3, 1)
        side[section, 1, j] = slope(m1 * v2, 0) + slope(m1 * v3, 1)
        cross = m3 * v2
        side[section, 2, j] = slope(m2 * v2 + press, 0) + slope(cross, 1)
        side[section, 3, j] = slope(cross, 0) + slope(m3 * v3 + press, 1) - rho * gravity
        side[section, 4, j] = slope(total * v2, 0) + slope(total * v3, 1) - m3 * gravity

    def begin(section, k):
        j = slot_of(k)
        for f in range(5):
            slope_one = -COEFS[2] * flux[section, f, j - 3 * way]
            for d in (1, 2):
                slope_one = slope_one + COEFS[d - 1] * (flux[section, f, j + d * way] - flux[section, f, j - d * way])
            new = state[section, f, j] - time_step * side[section, f, j] - time_way * slope_one
            if section == 1:
                new = 0.75 * state[0, f, j] + 0.25 * new
            if section == 2:
                new = (1.0 / 3.0) * state[0, f, j] + (2.0 / 3.0) * new
            partial[section, f] = new

    weights = (1.0, 0.25, 2.0 / 3.0)

    def finish(section, values):
        scale = (weights[section] * COEFS[2]) * time_way
        return [partial[section, f] - scale * values[f] for f in range(5)]

    def store_state(section, j, values):
        for f in range(5):
            state[section, f, j] = values[f]

    def store_final(k, out):
        j = slot_of(k)
        for f in range(5):
            final[f, (1 - c) * (5 - k) + c * k] = out[f]
        rho, m1, m2, m3, energy = out
        inverse = 1.0 / rho
        v1, v2, v3 = m1 * inverse, m2 * inverse, m3 * inverse
        kinetic = 0.5 * (m1 * v1 + m2 * v2 + m3 * v3)
        one, both = gam_one[j], gam_pinf[j]
        press = one * (energy - kinetic) - both
        speed = jnp.abs(v1) + jnp.abs(v2) + jnp.abs(v3)
        speed = speed + 3.0 * jnp.sqrt(((one + 1.0) * press + both) * inverse)
        speed = jnp.maximum(jnp.maximum(speed[:8], speed[8:16]), jnp.maximum(speed[16:24], speed[24:]))
        best[...] = jnp.maximum(best[...], speed)

    def step(k, fetched, sections, sides):
        for section in range(sections):
            begin(section, k - 3 - 3 * section)
        if fetched:
            for core in range(2):
                pltpu.make_async_remote_copy(
                    fields.at[:, pl.ds(0, 1)],
                    raw.at[:, pl.ds(0, 1), pl.ds(0, 16), :],
                    halo_send.at[0, 0],
                    halo_recv.at[k - 6, core],
                    device_id=me_sib,
                    device_id_type=MESH,
                ).wait_recv()
        values = first_flux(0, slot_of(k))
        for section in range(sections):
            inner = k - 3 - 3 * section
            new = finish(section, values)
            if section == 2:
                store_final(inner, new)
            else:
                store_state(section + 1, slot_of(inner), new)
                values = first_flux(section + 1, slot_of(inner))
        if sides:
            for section in range(min(sections + 1, 3)):
                side_of(section, slot_of(k - 3 * section))

    def cut_copy(section, start_here, start_there):
        return pltpu.make_async_remote_copy(
            flux.at[section, :, pl.ds(start_here, 3)],
            flux.at[section, :, pl.ds(start_there, 3)],
            cut_send.at[section],
            cut_recv.at[section],
            device_id=me_sib,
            device_id_type=MESH,
        )

    def cut(section):
        return cut_copy(section, 12 - 9 * c, 15 * c)

    best[...] = jnp.zeros((8, 128), jnp.float32)
    levels[0, rows, :] = own_level[...]
    level_wait = lambda n, core: pltpu.make_async_remote_copy(
        own_level, levels.at[n, pl.ds(0, 16), :], lev_send.at[0], lev_recv.at[n, core], device_id=me_sib, device_id_type=MESH
    ).wait_recv()
    level_wait(0, s)
    copies[1].wait()
    sib_copy.wait_recv()

    @pl.loop(-3, 6, unroll=3)
    def _(k):
        set_gamma(k, 0, (1 - c) * (5 - k) + c * (6 + k))

    @pl.loop(-3, 0)
    def _(k):
        first_flux(0, slot_of(k))

    @pl.loop(0, 3)
    def _(k):
        first_flux(0, slot_of(k))
        side_of(0, slot_of(k))

    hear(0)
    tell(1)

    @pl.loop(3, 6)
    def _(k):
        step(k, False, 1, True)

    cut(1).start()
    level_wait(1, 0)
    level_wait(1, 1)

    @pl.loop(6, 15, unroll=3)
    def _(k):
        set_gamma(k, 1, (1 - c) * (17 - k) + c * (k - 6))

    hear(1)
    tell(2)
    cut(1).wait_recv()

    @pl.loop(6, 9)
    def _(k):
        step(k, True, 2, True)

    cut(2).start()
    hear(2)
    tell(3)
    cut(2).wait_recv()

    @pl.loop(9, 12)
    def _(k):
        step(k, True, 3, True)

    @pl.loop(12, 15)
    def _(k):
        step(k, True, 3, False)

    best_src[0] = jnp.max(best[...], axis=0, keepdims=True)
    one = pltpu.make_async_remote_copy(
        best_src.at[0], best_sib, one_send.at[0], one_recv.at[0], device_id=me_sib, device_id_type=MESH
    )
    one.start()
    hear(3)
    one.wait_recv()
    best_src[1] = jnp.maximum(best_src[0], best_sib[...])

    offsets = [(a, b, d) for a in range(nx) for b in range(ny) for d in range(nz)][1:]
    far = lambda o: -(min(o[0], nx - o[0]) + min(o[1], ny - o[1]) + min(o[2], nz - o[2]))
    offsets.sort(key=lambda o: (not (o[0] <= 1 and o[1] <= 1 and o[2] <= 1), far(o)))
    for i, (a, b, d) in enumerate(offsets):
        pltpu.make_async_remote_copy(
            best_src.at[1],
            best_all.at[i],
            all_send.at[0],
            all_recv.at[0],
            device_id=(lax.rem(x + a, nx), lax.rem(y + b, ny), lax.rem(z + d, nz), c),
            device_id_type=MESH,
        ).start()

    keep = pltpu.make_async_copy(
        final.at[:, :, rows, :], advanced.at[:, pl.ds(HALF * c, HALF)], out_sem.at[0]
    )
    keep.start()
    give = pltpu.make_async_remote_copy(
        final.at[:, :, pl.ds(pl.multiple_of(16 * s, 16), 16), :],
        advanced.at[:, pl.ds(HALF * c, HALF)],
        out_send.at[0],
        out_recv.at[0],
        device_id=me_sib,
        device_id_type=MESH,
    )
    give.start()

    for copy in level_copies:
        copy.wait_send()
    sib_copy.wait_send()
    for i in range(HALO):
        for toward in range(2):
            halo_copy(i, toward).wait_send()
    cut(1).wait_send()
    cut(2).wait_send()
    one.wait_send()
    keep.wait()
    give.wait()

    everything = pltpu.make_async_remote_copy(
        best_all, best_all, all_send.at[0], all_recv.at[0], device_id=me_sib, device_id_type=MESH
    )
    everything.wait_recv()
    largest = jnp.maximum(best_src[1], jnp.max(best_all[...], axis=0))
    next_speed[...] = jnp.broadcast_to(jnp.max(largest, axis=1, keepdims=True), (1, 128))
    everything.wait_send()


def keep_kernel(adv, spd, adv_out, spd_out, spd_s, sem):
    one = pltpu.make_async_copy(adv, adv_out, sem.at[0])
    spd_s[0] = spd[0, 0]
    two = pltpu.make_async_copy(spd_s, spd_out, sem.at[1])
    one.start(); two.start(); one.wait(); two.wait()


def solution(mesh, dims=DIMS):
    cores = mesh.shape["gy"]
    finer = Mesh(mesh.devices.reshape(*dims, cores), AXES)
    chips = dims[0] * dims[1] * dims[2]
    dma = pltpu.SemaphoreType.DMA
    f32 = jnp.float32

    def local(fields, phase_map, lagged_speed, step_count):
        adv, spd = pl.pallas_call(
            functools.partial(kernel, dims),
            out_shape=(
                jax.ShapeDtypeStruct(fields.shape, f32),
                jax.ShapeDtypeStruct((1, 128), f32),
            ),
            in_specs=[pl.BlockSpec(memory_space=pl.ANY)] * 4,
            out_specs=(pl.BlockSpec(memory_space=pl.ANY), pl.BlockSpec(memory_space=pltpu.VMEM)),
            scratch_shapes=[
                pltpu.VMEM((3, 5, SLOTS, 32, 128), f32),
                pltpu.VMEM((3, 5, SLOTS, 32, 128), f32),
                pltpu.VMEM((3, 5, SLOTS, 32, 128), f32),
                pltpu.VMEM((SLOTS, 32, 128), f32),
                pltpu.VMEM((SLOTS, 32, 128), f32),
                pltpu.VMEM((5, HALF, 32, 128), f32),
                pltpu.VMEM((3, 5, 32, 128), f32),
                pltpu.VMEM((PLANES, 16, 128), jnp.int32),
                pltpu.VMEM((16, 128), f32),
                pltpu.VMEM((2, 32, 128), f32),
                pltpu.SMEM((1,), f32),
                pltpu.SMEM((1,), jnp.int32),
                pltpu.VMEM((8, 128), f32),
                pltpu.VMEM((1, 128), f32),
                pltpu.VMEM((2, 1, 128), f32),
                pltpu.VMEM((chips - 1, 1, 128), f32),
                dma((5,)),
                dma((HALO, 2)),
                dma((HALO, 2)),
                dma((1,)),
                dma((1,)),
                dma((3,)),
                dma((2, 2)),
                dma((3,)),
                dma((3,)),
                dma((1,)),
                dma((1,)),
                dma((1,)),
                dma((1,)),
                dma((1,)),
                dma((1,)),
                dma((1,)),
                pltpu.SemaphoreType.REGULAR((4,)),
            ],
            compiler_params=pltpu.CompilerParams(
                collective_id=0, has_side_effects=True, vmem_limit_bytes=32 << 20
            ),
            name="step",
        )(pltpu.with_memory_space_constraint(fields, pltpu.HBM), pltpu.with_memory_space_constraint(phase_map, pltpu.HBM), lagged_speed, step_count)
        return pl.pallas_call(
            keep_kernel,
            out_shape=(jax.ShapeDtypeStruct(fields.shape, f32), jax.ShapeDtypeStruct((1,), f32)),
            in_specs=[pl.BlockSpec(memory_space=pl.ANY), pl.BlockSpec(memory_space=pltpu.VMEM)],
            out_specs=(pl.BlockSpec(memory_space=pltpu.HBM), pl.BlockSpec(memory_space=pltpu.HBM)),
            scratch_shapes=[pltpu.SMEM((1,), f32), dma((2,))],
            compiler_params=pltpu.CompilerParams(vmem_limit_bytes=1 << 20),
            name="keep",
        )(adv, spd)

    in_specs = (P(None, GX, "gy", None), P(GX, "gy", None), P(), P())
    out_specs = (P(None, GX, "gy", None), P())
    return jax.shard_map(local, mesh=finer, in_specs=in_specs, out_specs=out_specs, check_vma=False)
```

```python
import functools
import math

import jax
import jax.numpy as jnp
from jax import lax
from jax.experimental import pallas as pl
from jax.experimental.pallas import tpu as pltpu
from jax.sharding import Mesh
from jax.sharding import PartitionSpec as P

PERIOD = 64
DIMS = (4, 4, 8)
AXES = ("gx_0", "gx_1", "gx_2", "gy")
GX = AXES[:3]
MESH = pl.DeviceIdType.MESH

PLANES = 12
HALF = 6
HALO = 9
SLOTS = 18
COEFS = (0.75, -0.15, 1.0 / 60.0)


def slope(values, axis):
    size = values.shape[axis]
    total = None
    for d, coef in enumerate(COEFS, 1):
        term = coef * (pltpu.roll(values, size - d, axis) - pltpu.roll(values, d, axis))
        total = term if total is None else total + term
    return total


def cosine_of_step(step):
    u = (step % PERIOD - PERIOD // 2).astype(jnp.float32) * (2.0 * math.pi / PERIOD)
    half = 0.5 * u
    square = half * half
    sine = jnp.full_like(u, 0.0)
    for n in range(8, -1, -1):
        sine = sine * square + (-1.0) ** n / math.factorial(2 * n + 1)
    sine = sine * half
    return 2.0 * sine * sine - 1.0


def kernel(
    dims,
    fields, phase_map, lagged_speed, step_count,
    advanced, next_speed,
    state, flux, side, gam_one, gam_pinf, final, partial, phases, own_level, levels,
    speed_s, step_s, best, best_sib, best_src, best_all,
    loc_sem, halo_send, halo_recv, sib_send, sib_recv, lev_send, lev_recv,
    cut_send, cut_recv, out_sem, out_send, out_recv, one_send, one_recv, all_send, all_recv, know,
):
    nx, ny, nz = dims
    x, y, z, c = (lax.axis_index(a) for a in AXES)
    s = 1 - c
    chips = nx * ny * nz
    g = (x * ny + y) * nz + z

    def chip(index):
        return (index // (ny * nz), lax.rem(index // nz, ny), lax.rem(index, nz))

    right = chip(lax.rem(g + 1, chips))
    left = chip(lax.rem(g + chips - 1, chips))
    me_sib = (x, y, z, s)

    steps = ((1, 0, 0), (nx - 1, 0, 0), (0, 1, 0), (0, ny - 1, 0), (0, 0, 1), (0, 0, nz - 1))

    def away(a, b, d):
        return (lax.rem(x + a, nx), lax.rem(y + b, ny), lax.rem(z + d, nz), c)

    rounds = (
        [away(*step) for step in steps],
        [away(0, 0, 2 % nz), away(0, 0, (nz - 2) % nz)],
        [away(d, 0, 0) for d in range(1, nx)],
        [away(0, d, 0) for d in range(1, ny)],
    )

    def tell(i):
        for peer in rounds[i]:
            pl.semaphore_signal(know.at[i], inc=1, device_id=peer, device_id_type=MESH)

    def hear(i):
        pl.semaphore_wait(know.at[i], len(rounds[i]))

    barrier = pltpu.get_barrier_semaphore()
    mine = tuple(c * r + s * l for r, l in zip(right, left))
    peers = [(*mine, 0), (*mine, 1), me_sib] + rounds[0]
    for peer in peers:
        pl.semaphore_signal(barrier, inc=1, device_id=peer, device_id_type=MESH)

    row0 = pl.multiple_of(16 * c, 16)
    raw = state.at[0]
    copies = [
        pltpu.make_async_copy(phase_map, phases, loc_sem.at[0]),
        pltpu.make_async_copy(
            fields.at[:, pl.ds(3 * c, HALO)],
            raw.at[:, pl.ds(9 - 9 * c, HALO), pl.ds(row0, 16), :],
            loc_sem.at[1],
        ),
        pltpu.make_async_copy(lagged_speed, speed_s, loc_sem.at[2]),
        pltpu.make_async_copy(step_count, step_s, loc_sem.at[3]),
    ]
    for copy in copies:
        copy.start()
    copies[0].wait()
    lane = lax.broadcasted_iota(jnp.int32, (16, 128), 1)
    tile = jnp.zeros((16, 128), jnp.float32)
    for p in range(PLANES):
        level = jnp.sum(phases[p].astype(jnp.float32), axis=1, keepdims=True)
        tile = jnp.where(lane == p, level, tile)
    own_level[...] = tile

    pl.semaphore_wait(barrier, len(peers))

    rows = pl.ds(row0, 16)
    level_copies = [
        pltpu.make_async_remote_copy(
            own_level, levels.at[n, rows, :], lev_send.at[i], lev_recv.at[n, c], device_id=dev, device_id_type=MESH
        )
        for i, (n, dev) in enumerate(((0, me_sib), (1, (*right, 0)), (1, (*left, 1))))
    ]
    for copy in level_copies:
        copy.start()
    sib_copy = pltpu.make_async_remote_copy(
        fields.at[:, pl.ds(3 * s, HALO)],
        raw.at[:, pl.ds(9 - 9 * s, HALO), rows, :],
        sib_send.at[0],
        sib_recv.at[0],
        device_id=me_sib,
        device_id_type=MESH,
    )

    def halo_copy(i, toward):
        src, slot, dev = ((11 - i, 8 - i, (*right, 0)), (i, 9 + i, (*left, 1)))[toward]
        return pltpu.make_async_remote_copy(
            fields.at[:, pl.ds(src, 1)],
            raw.at[:, pl.ds(slot, 1), rows, :],
            halo_send.at[i, toward],
            halo_recv.at[i, c],
            device_id=dev,
            device_id_type=MESH,
        )

    for toward in range(2):
        halo_copy(0, toward).start()
    sib_copy.start()
    for i in range(1, HALO):
        for toward in range(2):
            halo_copy(i, toward).start()
    tell(0)

    copies[2].wait()
    copies[3].wait()
    time_step = 0.9 / jnp.full((8, 128), speed_s[0], jnp.float32)
    gravity = 1.0 + 0.8 * cosine_of_step(jnp.full((8, 128), step_s[0], jnp.int32))
    time_step = jnp.concatenate([time_step] * 4, axis=0)
    gravity = jnp.concatenate([gravity] * 4, axis=0)
    way = 2 * c - 1
    time_way = time_step * way.astype(jnp.float32)

    lane32 = lax.broadcasted_iota(jnp.int32, (32, 128), 1)

    def slot_of(k):
        return 14 - k + c * (2 * k - 11)

    def set_gamma(k, n, plane):
        chosen = jnp.where(lane32 == plane, levels[n], 0.0)
        level = jnp.sum(chosen, axis=1, keepdims=True)
        water = jnp.where(lane32.astype(jnp.float32) < level, 1.0, 0.0)
        gamma = 1.4 + 3.0 * water
        j = slot_of(k)
        gam_one[j] = gamma - 1.0
        gam_pinf[j] = gamma * (3.0 * water)

    def primitives(section, j):
        rho, m1, m2, m3, energy = (state[section, f, j] for f in range(5))
        inverse = 1.0 / rho
        v1, v2, v3 = m1 * inverse, m2 * inverse, m3 * inverse
        kinetic = 0.5 * (m1 * v1 + m2 * v2 + m3 * v3)
        press = gam_one[j] * (energy - kinetic) - gam_pinf[j]
        return rho, (m1, m2, m3), (v1, v2, v3), press, energy + press

    def first_flux(section, j):
        _, (m1, m2, m3), (v1, _, _), press, total = primitives(section, j)
        values = (m1, m1 * v1 + press, m2 * v1, m3 * v1, total * v1)
        for f in range(5):
            flux[section, f, j] = values[f]
        return values

    def side_of(section, j):
        rho, (m1, m2, m3), (_, v2, v3), press, total = primitives(section, j)
        side[section, 0, j] = slope(m2, 0) + slope(m3, 1)
        side[section, 1, j] = slope(m1 * v2, 0) + slope(m1 * v3, 1)
        cross = m3 * v2
        side[section, 2, j] = slope(m2 * v2 + press, 0) + slope(cross, 1)
        side[section, 3, j] = slope(cross, 0) + slope(m3 * v3 + press, 1) - rho * gravity
        side[section, 4, j] = slope(total * v2, 0) + slope(total * v3, 1) - m3 * gravity

    def begin(section, k):
        j = slot_of(k)
        for f in range(5):
            slope_one = -COEFS[2] * flux[section, f, j - 3 * way]
            for d in (1, 2):
                slope_one = slope_one + COEFS[d - 1] * (flux[section, f, j + d * way] - flux[section, f, j - d * way])
            new = state[section, f, j] - time_step * side[section, f, j] - time_way * slope_one
            if section == 1:
                new = 0.75 * state[0, f, j] + 0.25 * new
            if section == 2:
                new = (1.0 / 3.0) * state[0, f, j] + (2.0 / 3.0) * new
            partial[section, f] = new

    weights = (1.0, 0.25, 2.0 / 3.0)

    def finish(section, values):
        scale = (weights[section] * COEFS[2]) * time_way
        return [partial[section, f] - scale * values[f] for f in range(5)]

    def store_state(section, j, values):
        for f in range(5):
            state[section, f, j] = values[f]

    def store_final(k, out):
        j = slot_of(k)
        for f in range(5):
            final[f, (1 - c) * (5 - k) + c * k] = out[f]
        rho, m1, m2, m3, energy = out
        inverse = 1.0 / rho
        v1, v2, v3 = m1 * inverse, m2 * inverse, m3 * inverse
        kinetic = 0.5 * (m1 * v1 + m2 * v2 + m3 * v3)
        one, both = gam_one[j], gam_pinf[j]
        press = one * (energy - kinetic) - both
        speed = jnp.abs(v1) + jnp.abs(v2) + jnp.abs(v3)
        speed = speed + 3.0 * jnp.sqrt(((one + 1.0) * press + both) * inverse)
        speed = jnp.maximum(jnp.maximum(speed[:8], speed[8:16]), jnp.maximum(speed[16:24], speed[24:]))
        best[...] = jnp.maximum(best[...], speed)

    def step(k, fetched, sections, sides):
        for section in range(sections):
            begin(section, k - 3 - 3 * section)
        if fetched:
            for core in range(2):
                pltpu.make_async_remote_copy(
                    fields.at[:, pl.ds(0, 1)],
                    raw.at[:, pl.ds(0, 1), pl.ds(0, 16), :],
                    halo_send.at[0, 0],
                    halo_recv.at[k - 6, core],
                    device_id=me_sib,
                    device_id_type=MESH,
                ).wait_recv()
        values = first_flux(0, slot_of(k))
        for section in range(sections):
            inner = k - 3 - 3 * section
            new = finish(section, values)
            if section == 2:
                store_final(inner, new)
            else:
                store_state(section + 1, slot_of(inner), new)
                values = first_flux(section + 1, slot_of(inner))
        if sides:
            for section in range(min(sections + 1, 3)):
                side_of(section, slot_of(k - 3 * section))

    def cut_copy(section, start_here, start_there):
        return pltpu.make_async_remote_copy(
            flux.at[section, :, pl.ds(start_here, 3)],
            flux.at[section, :, pl.ds(start_there, 3)],
            cut_send.at[section],
            cut_recv.at[section],
            device_id=me_sib,
            device_id_type=MESH,
        )

    def cut(section):
        return cut_copy(section, 12 - 9 * c, 15 * c)

    best[...] = jnp.zeros((8, 128), jnp.float32)
    levels[0, rows, :] = own_level[...]
    level_wait = lambda n, core: pltpu.make_async_remote_copy(
        own_level, levels.at[n, pl.ds(0, 16), :], lev_send.at[0], lev_recv.at[n, core], device_id=me_sib, device_id_type=MESH
    ).wait_recv()
    level_wait(0, s)
    copies[1].wait()
    sib_copy.wait_recv()

    @pl.loop(-3, 6, unroll=3)
    def _(k):
        set_gamma(k, 0, (1 - c) * (5 - k) + c * (6 + k))

    @pl.loop(-3, 0)
    def _(k):
        first_flux(0, slot_of(k))

    @pl.loop(0, 3)
    def _(k):
        first_flux(0, slot_of(k))
        side_of(0, slot_of(k))

    hear(0)
    tell(1)

    @pl.loop(3, 6)
    def _(k):
        step(k, False, 1, True)

    cut(1).start()
    level_wait(1, 0)
    level_wait(1, 1)

    @pl.loop(6, 15, unroll=3)
    def _(k):
        set_gamma(k, 1, (1 - c) * (17 - k) + c * (k - 6))

    hear(1)
    tell(2)
    cut(1).wait_recv()

    @pl.loop(6, 9)
    def _(k):
        step(k, True, 2, True)

    cut(2).start()
    hear(2)
    tell(3)
    cut(2).wait_recv()

    @pl.loop(9, 12)
    def _(k):
        step(k, True, 3, True)

    @pl.loop(12, 15, unroll=3)
    def _(k):
        step(k, True, 3, False)

    best_src[0] = jnp.max(best[...], axis=0, keepdims=True)
    one = pltpu.make_async_remote_copy(
        best_src.at[0], best_sib, one_send.at[0], one_recv.at[0], device_id=me_sib, device_id_type=MESH
    )
    one.start()
    hear(3)
    one.wait_recv()
    best_src[1] = jnp.maximum(best_src[0], best_sib[...])

    offsets = [(a, b, d) for a in range(nx) for b in range(ny) for d in range(nz)][1:]
    far = lambda o: -(min(o[0], nx - o[0]) + min(o[1], ny - o[1]) + min(o[2], nz - o[2]))
    offsets.sort(key=lambda o: (not (o[0] <= 1 and o[1] <= 1 and o[2] <= 1), far(o)))
    along_x = [lax.rem(x + a, nx) * (2 * ny * nz) for a in range(nx)]
    along_y = [lax.rem(y + b, ny) * (2 * nz) + c for b in range(ny)]
    along_z = [lax.rem(z + d, nz) * 2 for d in range(nz)]
    for i, (a, b, d) in enumerate(offsets):
        pltpu.make_async_remote_copy(
            best_src.at[1],
            best_all.at[i],
            all_send.at[0],
            all_recv.at[0],
            device_id=along_x[a] + along_y[b] + along_z[d],
            device_id_type=pl.DeviceIdType.LOGICAL,
        ).start()

    keep = pltpu.make_async_copy(
        final.at[:, :, rows, :], advanced.at[:, pl.ds(HALF * c, HALF)], out_sem.at[0]
    )
    keep.start()
    give = pltpu.make_async_remote_copy(
        final.at[:, :, pl.ds(pl.multiple_of(16 * s, 16), 16), :],
        advanced.at[:, pl.ds(HALF * c, HALF)],
        out_send.at[0],
        out_recv.at[0],
        device_id=me_sib,
        device_id_type=MESH,
    )
    give.start()

    for copy in level_copies:
        copy.wait_send()
    sib_copy.wait_send()
    for i in range(HALO):
        for toward in range(2):
            halo_copy(i, toward).wait_send()
    cut(1).wait_send()
    cut(2).wait_send()
    one.wait_send()
    keep.wait()
    give.wait()

    everything = pltpu.make_async_remote_copy(
        best_all, best_all, all_send.at[0], all_recv.at[0], device_id=me_sib, device_id_type=MESH
    )
    everything.wait_recv()
    largest = jnp.maximum(best_src[1], jnp.max(best_all[...], axis=0))
    next_speed[...] = jnp.broadcast_to(jnp.max(largest, axis=1, keepdims=True), (1, 128))
    everything.wait_send()


def keep_kernel(adv, spd, adv_out, spd_out, spd_s, sem):
    one = pltpu.make_async_copy(adv, adv_out, sem.at[0])
    spd_s[0] = spd[0, 0]
    two = pltpu.make_async_copy(spd_s, spd_out, sem.at[1])
    one.start(); two.start(); one.wait(); two.wait()


def solution(mesh, dims=DIMS):
    cores = mesh.shape["gy"]
    finer = Mesh(mesh.devices.reshape(*dims, cores), AXES)
    chips = dims[0] * dims[1] * dims[2]
    dma = pltpu.SemaphoreType.DMA
    f32 = jnp.float32

    def local(fields, phase_map, lagged_speed, step_count):
        adv, spd = pl.pallas_call(
            functools.partial(kernel, dims),
            out_shape=(
                jax.ShapeDtypeStruct(fields.shape, f32),
                jax.ShapeDtypeStruct((1, 128), f32),
            ),
            in_specs=[pl.BlockSpec(memory_space=pl.ANY)] * 4,
            out_specs=(pl.BlockSpec(memory_space=pl.ANY), pl.BlockSpec(memory_space=pltpu.VMEM)),
            scratch_shapes=[
                pltpu.VMEM((3, 5, SLOTS, 32, 128), f32),
                pltpu.VMEM((3, 5, SLOTS, 32, 128), f32),
                pltpu.VMEM((3, 5, SLOTS, 32, 128), f32),
                pltpu.VMEM((SLOTS, 32, 128), f32),
                pltpu.VMEM((SLOTS, 32, 128), f32),
                pltpu.VMEM((5, HALF, 32, 128), f32),
                pltpu.VMEM((3, 5, 32, 128), f32),
                pltpu.VMEM((PLANES, 16, 128), jnp.int32),
                pltpu.VMEM((16, 128), f32),
                pltpu.VMEM((2, 32, 128), f32),
                pltpu.SMEM((1,), f32),
                pltpu.SMEM((1,), jnp.int32),
                pltpu.VMEM((8, 128), f32),
                pltpu.VMEM((1, 128), f32),
                pltpu.VMEM((2, 1, 128), f32),
                pltpu.VMEM((chips - 1, 1, 128), f32),
                dma((5,)),
                dma((HALO, 2)),
                dma((HALO, 2)),
                dma((1,)),
                dma((1,)),
                dma((3,)),
                dma((2, 2)),
                dma((3,)),
                dma((3,)),
                dma((1,)),
                dma((1,)),
                dma((1,)),
                dma((1,)),
                dma((1,)),
                dma((1,)),
                dma((1,)),
                pltpu.SemaphoreType.REGULAR((4,)),
            ],
            compiler_params=pltpu.CompilerParams(
                collective_id=0, has_side_effects=True, vmem_limit_bytes=32 << 20
            ),
            name="step",
        )(pltpu.with_memory_space_constraint(fields, pltpu.HBM), pltpu.with_memory_space_constraint(phase_map, pltpu.HBM), lagged_speed, step_count)
        return pl.pallas_call(
            keep_kernel,
            out_shape=(jax.ShapeDtypeStruct(fields.shape, f32), jax.ShapeDtypeStruct((1,), f32)),
            in_specs=[pl.BlockSpec(memory_space=pl.ANY), pl.BlockSpec(memory_space=pltpu.VMEM)],
            out_specs=(pl.BlockSpec(memory_space=pltpu.HBM), pl.BlockSpec(memory_space=pltpu.HBM)),
            scratch_shapes=[pltpu.SMEM((1,), f32), dma((2,))],
            compiler_params=pltpu.CompilerParams(vmem_limit_bytes=1 << 20),
            name="keep",
        )(adv, spd)

    in_specs = (P(None, GX, "gy", None), P(GX, "gy", None), P(), P())
    out_specs = (P(None, GX, "gy", None), P())
    return jax.shard_map(local, mesh=finer, in_specs=in_specs, out_specs=out_specs, check_vma=False)
```

```python
import functools
import math

import jax
import jax.numpy as jnp
from jax import lax
from jax.experimental import pallas as pl
from jax.experimental.pallas import tpu as pltpu
from jax.sharding import Mesh
from jax.sharding import PartitionSpec as P

PERIOD = 64
DIMS = (4, 4, 8)
AXES = ("gx_0", "gx_1", "gx_2", "gy")
GX = AXES[:3]
MESH = pl.DeviceIdType.MESH

PLANES = 12
HALF = 6
HALO = 9
SPLIT = 6
SLOTS = 18
COEFS = (0.75, -0.15, 1.0 / 60.0)


def slope(values, axis):
    size = values.shape[axis]
    total = None
    for d, coef in enumerate(COEFS, 1):
        term = coef * (pltpu.roll(values, size - d, axis) - pltpu.roll(values, d, axis))
        total = term if total is None else total + term
    return total


def cosine_of_step(step):
    u = (step % PERIOD - PERIOD // 2).astype(jnp.float32) * (2.0 * math.pi / PERIOD)
    half = 0.5 * u
    square = half * half
    sine = jnp.full_like(u, 0.0)
    for n in range(8, -1, -1):
        sine = sine * square + (-1.0) ** n / math.factorial(2 * n + 1)
    sine = sine * half
    return 2.0 * sine * sine - 1.0


def kernel(
    dims,
    fields, phase_map, lagged_speed, step_count,
    advanced, next_speed,
    state, flux, side, gam_one, gam_pinf, final, partial, phases, own_level, levels,
    speed_s, step_s, best, best_sib, best_src, best_all,
    loc_sem, halo_send, halo_recv, sib_send, sib_recv, lev_send, lev_recv,
    cut_send, cut_recv, out_sem, out_send, out_recv, one_send, one_recv, all_send, all_recv, know,
):
    nx, ny, nz = dims
    x, y, z, c = (lax.axis_index(a) for a in AXES)
    s = 1 - c
    chips = nx * ny * nz
    g = (x * ny + y) * nz + z

    def chip(index):
        return (index // (ny * nz), lax.rem(index // nz, ny), lax.rem(index, nz))

    right = chip(lax.rem(g + 1, chips))
    left = chip(lax.rem(g + chips - 1, chips))
    me_sib = (x, y, z, s)

    steps = ((1, 0, 0), (nx - 1, 0, 0), (0, 1, 0), (0, ny - 1, 0), (0, 0, 1), (0, 0, nz - 1))

    def away(a, b, d):
        return (lax.rem(x + a, nx), lax.rem(y + b, ny), lax.rem(z + d, nz), c)

    rounds = (
        [away(*step) for step in steps],
        [away(0, 0, 2 % nz), away(0, 0, (nz - 2) % nz)],
        [away(d, 0, 0) for d in range(1, nx)],
        [away(0, d, 0) for d in range(1, ny)],
    )

    def tell(i):
        for peer in rounds[i]:
            pl.semaphore_signal(know.at[i], inc=1, device_id=peer, device_id_type=MESH)

    def hear(i):
        pl.semaphore_wait(know.at[i], len(rounds[i]))

    barrier = pltpu.get_barrier_semaphore()
    mine = tuple(c * r + s * l for r, l in zip(right, left))
    peers = [(*mine, 0), (*mine, 1), me_sib] + rounds[0]
    for peer in peers:
        pl.semaphore_signal(barrier, inc=1, device_id=peer, device_id_type=MESH)

    row0 = pl.multiple_of(16 * c, 16)
    raw = state.at[0]
    copies = [
        pltpu.make_async_copy(phase_map, phases, loc_sem.at[0]),
        pltpu.make_async_copy(
            fields.at[:, pl.ds(3 * c, HALO)],
            raw.at[:, pl.ds(9 - 9 * c, HALO), pl.ds(row0, 16), :],
            loc_sem.at[1],
        ),
        pltpu.make_async_copy(lagged_speed, speed_s, loc_sem.at[2]),
        pltpu.make_async_copy(step_count, step_s, loc_sem.at[3]),
    ]
    for copy in copies:
        copy.start()
    copies[0].wait()
    lane = lax.broadcasted_iota(jnp.int32, (16, 128), 1)
    tile = jnp.zeros((16, 128), jnp.float32)
    for p in range(PLANES):
        level = jnp.sum(phases[p].astype(jnp.float32), axis=1, keepdims=True)
        tile = jnp.where(lane == p, level, tile)
    own_level[...] = tile

    pl.semaphore_wait(barrier, len(peers))

    rows = pl.ds(row0, 16)
    level_copies = [
        pltpu.make_async_remote_copy(
            own_level, levels.at[n, rows, :], lev_send.at[i], lev_recv.at[n, c], device_id=dev, device_id_type=MESH
        )
        for i, (n, dev) in enumerate(((0, me_sib), (1, (*right, 0)), (1, (*left, 1))))
    ]
    for copy in level_copies:
        copy.start()
    sib_copy = pltpu.make_async_remote_copy(
        fields.at[:, pl.ds(3 * s, HALO)],
        raw.at[:, pl.ds(9 - 9 * s, HALO), rows, :],
        sib_send.at[0],
        sib_recv.at[0],
        device_id=me_sib,
        device_id_type=MESH,
    )

    def halo_copy(i, toward):
        src, slot, dev = ((11 - i, 8 - i, (*right, 0)), (i, 9 + i, (*left, 1)))[toward]
        return pltpu.make_async_remote_copy(
            fields.at[:, pl.ds(src, 1)],
            raw.at[:, pl.ds(slot, 1), rows, :],
            halo_send.at[i, toward],
            halo_recv.at[i, c],
            device_id=dev,
            device_id_type=MESH,
        )

    for toward in range(2):
        halo_copy(0, toward).start()
    sib_copy.start()
    for i in range(1, SPLIT):
        for toward in range(2):
            halo_copy(i, toward).start()

    def whole_copy(i, toward):
        src, slot, dev = ((8 - i, 8 - i, (*right, 0)), (i - 3, 9 + i, (*left, 1)))[toward]
        return pltpu.make_async_remote_copy(
            raw.at[:, pl.ds(src, 1)],
            raw.at[:, pl.ds(slot, 1)],
            halo_send.at[i, toward],
            halo_recv.at[i, 1],
            device_id=dev,
            device_id_type=MESH,
        )
    tell(0)

    copies[2].wait()
    copies[3].wait()
    time_step = 0.9 / jnp.full((8, 128), speed_s[0], jnp.float32)
    gravity = 1.0 + 0.8 * cosine_of_step(jnp.full((8, 128), step_s[0], jnp.int32))
    time_step = jnp.concatenate([time_step] * 4, axis=0)
    gravity = jnp.concatenate([gravity] * 4, axis=0)
    way = 2 * c - 1
    time_way = time_step * way.astype(jnp.float32)

    lane32 = lax.broadcasted_iota(jnp.int32, (32, 128), 1)

    def slot_of(k):
        return 14 - k + c * (2 * k - 11)

    def set_gamma(k, n, plane):
        chosen = jnp.where(lane32 == plane, levels[n], 0.0)
        level = jnp.sum(chosen, axis=1, keepdims=True)
        water = jnp.where(lane32.astype(jnp.float32) < level, 1.0, 0.0)
        gamma = 1.4 + 3.0 * water
        j = slot_of(k)
        gam_one[j] = gamma - 1.0
        gam_pinf[j] = gamma * (3.0 * water)

    def primitives(section, j):
        rho, m1, m2, m3, energy = (state[section, f, j] for f in range(5))
        inverse = 1.0 / rho
        v1, v2, v3 = m1 * inverse, m2 * inverse, m3 * inverse
        kinetic = 0.5 * (m1 * v1 + m2 * v2 + m3 * v3)
        press = gam_one[j] * (energy - kinetic) - gam_pinf[j]
        return rho, (m1, m2, m3), (v1, v2, v3), press, energy + press

    def first_flux(section, j):
        _, (m1, m2, m3), (v1, _, _), press, total = primitives(section, j)
        values = (m1, m1 * v1 + press, m2 * v1, m3 * v1, total * v1)
        for f in range(5):
            flux[section, f, j] = values[f]
        return values

    def side_of(section, j):
        rho, (m1, m2, m3), (_, v2, v3), press, total = primitives(section, j)
        side[section, 0, j] = slope(m2, 0) + slope(m3, 1)
        side[section, 1, j] = slope(m1 * v2, 0) + slope(m1 * v3, 1)
        cross = m3 * v2
        side[section, 2, j] = slope(m2 * v2 + press, 0) + slope(cross, 1)
        side[section, 3, j] = slope(cross, 0) + slope(m3 * v3 + press, 1) - rho * gravity
        side[section, 4, j] = slope(total * v2, 0) + slope(total * v3, 1) - m3 * gravity

    def begin(section, k):
        j = slot_of(k)
        for f in range(5):
            slope_one = -COEFS[2] * flux[section, f, j - 3 * way]
            for d in (1, 2):
                slope_one = slope_one + COEFS[d - 1] * (flux[section, f, j + d * way] - flux[section, f, j - d * way])
            new = state[section, f, j] - time_step * side[section, f, j] - time_way * slope_one
            if section == 1:
                new = 0.75 * state[0, f, j] + 0.25 * new
            if section == 2:
                new = (1.0 / 3.0) * state[0, f, j] + (2.0 / 3.0) * new
            partial[section, f] = new

    weights = (1.0, 0.25, 2.0 / 3.0)

    def finish(section, values):
        scale = (weights[section] * COEFS[2]) * time_way
        return [partial[section, f] - scale * values[f] for f in range(5)]

    def store_state(section, j, values):
        for f in range(5):
            state[section, f, j] = values[f]

    def store_final(k, out):
        j = slot_of(k)
        for f in range(5):
            final[f, (1 - c) * (5 - k) + c * k] = out[f]
        rho, m1, m2, m3, energy = out
        inverse = 1.0 / rho
        v1, v2, v3 = m1 * inverse, m2 * inverse, m3 * inverse
        kinetic = 0.5 * (m1 * v1 + m2 * v2 + m3 * v3)
        one, both = gam_one[j], gam_pinf[j]
        press = one * (energy - kinetic) - both
        speed = jnp.abs(v1) + jnp.abs(v2) + jnp.abs(v3)
        speed = speed + 3.0 * jnp.sqrt(((one + 1.0) * press + both) * inverse)
        speed = jnp.maximum(jnp.maximum(speed[:8], speed[8:16]), jnp.maximum(speed[16:24], speed[24:]))
        best[...] = jnp.maximum(best[...], speed)

    def step(k, fetched, sections, sides):
        for section in range(sections):
            begin(section, k - 3 - 3 * section)
        if fetched == 2:
            whole = raw.at[:, pl.ds(0, 1)]
            pltpu.make_async_remote_copy(
                whole, whole, halo_send.at[0, 0], halo_recv.at[k - 6, 1], device_id=me_sib, device_id_type=MESH
            ).wait_recv()
        if fetched == 1:
            for core in range(2):
                pltpu.make_async_remote_copy(
                    fields.at[:, pl.ds(0, 1)],
                    raw.at[:, pl.ds(0, 1), pl.ds(0, 16), :],
                    halo_send.at[0, 0],
                    halo_recv.at[k - 6, core],
                    device_id=me_sib,
                    device_id_type=MESH,
                ).wait_recv()
        values = first_flux(0, slot_of(k))
        for section in range(sections):
            inner = k - 3 - 3 * section
            new = finish(section, values)
            if section == 2:
                store_final(inner, new)
            else:
                store_state(section + 1, slot_of(inner), new)
                values = first_flux(section + 1, slot_of(inner))
        if sides:
            for section in range(min(sections + 1, 3)):
                side_of(section, slot_of(k - 3 * section))

    def cut_copy(section, start_here, start_there):
        return pltpu.make_async_remote_copy(
            flux.at[section, :, pl.ds(start_here, 3)],
            flux.at[section, :, pl.ds(start_there, 3)],
            cut_send.at[section],
            cut_recv.at[section],
            device_id=me_sib,
            device_id_type=MESH,
        )

    def cut(section):
        return cut_copy(section, 12 - 9 * c, 15 * c)

    best[...] = jnp.zeros((8, 128), jnp.float32)
    levels[0, rows, :] = own_level[...]
    level_wait = lambda n, core: pltpu.make_async_remote_copy(
        own_level, levels.at[n, pl.ds(0, 16), :], lev_send.at[0], lev_recv.at[n, core], device_id=me_sib, device_id_type=MESH
    ).wait_recv()
    level_wait(0, s)
    copies[1].wait()
    sib_copy.wait_recv()

    @pl.when(c == 1)
    def _():
        for i in range(SPLIT, HALO):
            for toward in range(2):
                whole_copy(i, toward).start()


    @pl.loop(-3, 6, unroll=3)
    def _(k):
        set_gamma(k, 0, (1 - c) * (5 - k) + c * (6 + k))

    @pl.loop(-3, 0)
    def _(k):
        first_flux(0, slot_of(k))

    @pl.loop(0, 3)
    def _(k):
        first_flux(0, slot_of(k))
        side_of(0, slot_of(k))

    hear(0)
    tell(1)

    @pl.loop(3, 6)
    def _(k):
        step(k, 0, 1, True)

    cut(1).start()
    level_wait(1, 0)
    level_wait(1, 1)

    @pl.loop(6, 15, unroll=3)
    def _(k):
        set_gamma(k, 1, (1 - c) * (17 - k) + c * (k - 6))

    hear(1)
    tell(2)
    cut(1).wait_recv()

    @pl.loop(6, 9)
    def _(k):
        step(k, 1, 2, True)

    cut(2).start()
    hear(2)
    tell(3)
    cut(2).wait_recv()

    @pl.loop(9, 12)
    def _(k):
        step(k, 1, 3, True)

    @pl.loop(12, 15)
    def _(k):
        step(k, 2, 3, False)

    best_src[0] = jnp.max(best[...], axis=0, keepdims=True)
    one = pltpu.make_async_remote_copy(
        best_src.at[0], best_sib, one_send.at[0], one_recv.at[0], device_id=me_sib, device_id_type=MESH
    )
    one.start()
    hear(3)
    one.wait_recv()
    best_src[1] = jnp.maximum(best_src[0], best_sib[...])

    offsets = [(a, b, d) for a in range(nx) for b in range(ny) for d in range(nz)][1:]
    far = lambda o: -(min(o[0], nx - o[0]) + min(o[1], ny - o[1]) + min(o[2], nz - o[2]))
    offsets.sort(key=lambda o: (not (o[0] <= 1 and o[1] <= 1 and o[2] <= 1), far(o)))
    for i, (a, b, d) in enumerate(offsets):
        pltpu.make_async_remote_copy(
            best_src.at[1],
            best_all.at[i],
            all_send.at[0],
            all_recv.at[0],
            device_id=(lax.rem(x + a, nx), lax.rem(y + b, ny), lax.rem(z + d, nz), c),
            device_id_type=MESH,
        ).start()

    keep = pltpu.make_async_copy(
        final.at[:, :, rows, :], advanced.at[:, pl.ds(HALF * c, HALF)], out_sem.at[0]
    )
    keep.start()
    give = pltpu.make_async_remote_copy(
        final.at[:, :, pl.ds(pl.multiple_of(16 * s, 16), 16), :],
        advanced.at[:, pl.ds(HALF * c, HALF)],
        out_send.at[0],
        out_recv.at[0],
        device_id=me_sib,
        device_id_type=MESH,
    )
    give.start()

    for copy in level_copies:
        copy.wait_send()
    sib_copy.wait_send()
    for i in range(SPLIT):
        for toward in range(2):
            halo_copy(i, toward).wait_send()

    @pl.when(c == 1)
    def _():
        for i in range(SPLIT, HALO):
            for toward in range(2):
                whole_copy(i, toward).wait_send()

    cut(1).wait_send()
    cut(2).wait_send()
    one.wait_send()
    keep.wait()
    give.wait()

    everything = pltpu.make_async_remote_copy(
        best_all, best_all, all_send.at[0], all_recv.at[0], device_id=me_sib, device_id_type=MESH
    )
    everything.wait_recv()
    largest = jnp.maximum(best_src[1], jnp.max(best_all[...], axis=0))
    next_speed[...] = jnp.broadcast_to(jnp.max(largest, axis=1, keepdims=True), (1, 128))
    everything.wait_send()


def keep_kernel(adv, spd, adv_out, spd_out, spd_s, sem):
    one = pltpu.make_async_copy(adv, adv_out, sem.at[0])
    spd_s[0] = spd[0, 0]
    two = pltpu.make_async_copy(spd_s, spd_out, sem.at[1])
    one.start(); two.start(); one.wait(); two.wait()


def solution(mesh, dims=DIMS):
    cores = mesh.shape["gy"]
    finer = Mesh(mesh.devices.reshape(*dims, cores), AXES)
    chips = dims[0] * dims[1] * dims[2]
    dma = pltpu.SemaphoreType.DMA
    f32 = jnp.float32

    def local(fields, phase_map, lagged_speed, step_count):
        adv, spd = pl.pallas_call(
            functools.partial(kernel, dims),
            out_shape=(
                jax.ShapeDtypeStruct(fields.shape, f32),
                jax.ShapeDtypeStruct((1, 128), f32),
            ),
            in_specs=[pl.BlockSpec(memory_space=pl.ANY)] * 4,
            out_specs=(pl.BlockSpec(memory_space=pl.ANY), pl.BlockSpec(memory_space=pltpu.VMEM)),
            scratch_shapes=[
                pltpu.VMEM((3, 5, SLOTS, 32, 128), f32),
                pltpu.VMEM((3, 5, SLOTS, 32, 128), f32),
                pltpu.VMEM((3, 5, SLOTS, 32, 128), f32),
                pltpu.VMEM((SLOTS, 32, 128), f32),
                pltpu.VMEM((SLOTS, 32, 128), f32),
                pltpu.VMEM((5, HALF, 32, 128), f32),
                pltpu.VMEM((3, 5, 32, 128), f32),
                pltpu.VMEM((PLANES, 16, 128), jnp.int32),
                pltpu.VMEM((16, 128), f32),
                pltpu.VMEM((2, 32, 128), f32),
                pltpu.SMEM((1,), f32),
                pltpu.SMEM((1,), jnp.int32),
                pltpu.VMEM((8, 128), f32),
                pltpu.VMEM((1, 128), f32),
                pltpu.VMEM((2, 1, 128), f32),
                pltpu.VMEM((chips - 1, 1, 128), f32),
                dma((5,)),
                dma((HALO, 2)),
                dma((HALO, 2)),
                dma((1,)),
                dma((1,)),
                dma((3,)),
                dma((2, 2)),
                dma((3,)),
                dma((3,)),
                dma((1,)),
                dma((1,)),
                dma((1,)),
                dma((1,)),
                dma((1,)),
                dma((1,)),
                dma((1,)),
                pltpu.SemaphoreType.REGULAR((4,)),
            ],
            compiler_params=pltpu.CompilerParams(
                collective_id=0, has_side_effects=True, vmem_limit_bytes=32 << 20
            ),
            name="step",
        )(pltpu.with_memory_space_constraint(fields, pltpu.HBM), pltpu.with_memory_space_constraint(phase_map, pltpu.HBM), lagged_speed, step_count)
        return pl.pallas_call(
            keep_kernel,
            out_shape=(jax.ShapeDtypeStruct(fields.shape, f32), jax.ShapeDtypeStruct((1,), f32)),
            in_specs=[pl.BlockSpec(memory_space=pl.ANY), pl.BlockSpec(memory_space=pltpu.VMEM)],
            out_specs=(pl.BlockSpec(memory_space=pltpu.HBM), pl.BlockSpec(memory_space=pltpu.HBM)),
            scratch_shapes=[pltpu.SMEM((1,), f32), dma((2,))],
            compiler_params=pltpu.CompilerParams(vmem_limit_bytes=1 << 20),
            name="keep",
        )(adv, spd)

    in_specs = (P(None, GX, "gy", None), P(GX, "gy", None), P(), P())
    out_specs = (P(None, GX, "gy", None), P())
    return jax.shard_map(local, mesh=finer, in_specs=in_specs, out_specs=out_specs, check_vma=False)
```
